128 devices in a mesh: ctx: 16 (over y, x_lo, core), head: 8 (over z, x_hi).
Axes of the slice: x: 4 (x_hi: 2, x_lo: 2; x = x_hi * 2 + x_lo), y: 4, z: 4, core: 2. Of those that a mesh axis runs over, the one named last changes fastest.
Arguments:
- q_prompt: bfloat16 [8192, 32, 256], P('ctx', 'head'), may hold values from -0.3984375 to 0.3984375
- k_prompt: bfloat16 [8192, 32, 256], P('ctx', 'head'), may hold values from -0.3984375 to 0.3984375
- v_prompt: bfloat16 [8192, 32, 256], P('ctx', 'head'), may hold values from -6 to 6
- log_decay: float32 [32, 8192], P('head', 'ctx'), may hold values from -1 to 0
- prompt_section: int32 [512, 1], P('ctx'), may hold values from 0 to 15; in each aligned block of 32 rows (0 to 31, 32 to 63, ...) at most 4 rows name the same one
- q_step: bfloat16 [512, 4, 32, 256], P('ctx', None, 'head'), may hold values from -0.3984375 to 0.3984375
- k_step: bfloat16 [512, 4, 32, 256], P('ctx', None, 'head'), may hold values from -3 to 3
- v_step: bfloat16 [512, 4, 32, 256], P('ctx', None, 'head'), may hold values from -6 to 6
- step_decay: float32 [32, 4, 512], P('head', None, 'ctx'), may hold values from -0.6 to -0.05
- w_out: bfloat16 [8192, 8192], P(None, 'head'), may hold values from -0.0625 to 0.0625
Outputs:
- prompt_out: bfloat16 [8192, 8192], P('ctx', 'head')
- step_out: bfloat16 [512, 4, 8192], P('ctx', None, 'head')
The draws below stay inside these ranges and needn't reach their ends.
Inputs may be any that keep to these rules, and one draw needn't show every extreme that they name: `prompt_section`: among the rows of one index of ctx, no section is named more than 4 times.
All inputs are finite; a program needn't handle non-finite values.
Results may differ from the reference program's by a relative error of at most 0.015.
Values may be sent and summed in bfloat16 or wider, within the bound.
No kernel may reach another device: no remote copies, remote signals or barrier semaphores. Data moves between devices by JAX's collectives and lax.ppermute only.
A program may use at most 128 MiB of HBM per device.

```python
import math
import jax
import jax.numpy as jnp
import numpy as np
from jax import lax

D = 8192
RETENTION_HEADS = 32
HD = 256
BLOCK = 512
STEPS = 4
TOK_DEV = 512
ROWS_DEV = 32
CAP = 4
PROMPT_TOKENS = 8192
ROWS = 512
N_CTX = 16


def draw_log_decay(key, part):
    random_subkey_list = jax.random.split(key, 7)
    fast_share = 0.5
    head_draw = jax.random.uniform(random_subkey_list[0], (RETENTION_HEADS, 1), jnp.float32)
    is_fast = head_draw < fast_share
    fast_rate = jnp.exp(jax.random.uniform(random_subkey_list[1], (RETENTION_HEADS, 1), jnp.float32, jnp.log(1.0 / 50.0), jnp.log(1.0 / 30.0)))
    slow_rate = jnp.exp(jax.random.uniform(random_subkey_list[2], (RETENTION_HEADS, 1), jnp.float32, jnp.log(0.1), jnp.log(0.5))) / PROMPT_TOKENS
    baseline_decay_rate = jnp.where(is_fast, fast_rate, slow_rate)
    rough_decay = jnp.exp(jax.random.uniform(random_subkey_list[3], (RETENTION_HEADS, 64), jnp.float32, jnp.log(0.5), jnp.log(2.0)))
    rough_decay = jnp.repeat(rough_decay, PROMPT_TOKENS // 64, axis=1)
    random_wobble = jax.random.uniform(random_subkey_list[4], (RETENTION_HEADS, PROMPT_TOKENS), jnp.float32, 0.5, 1.5)
    decay_spikes = jax.random.uniform(random_subkey_list[5], (RETENTION_HEADS, PROMPT_TOKENS), jnp.float32) < 3.0 / PROMPT_TOKENS
    spike_log_decay = jnp.log(jax.random.uniform(random_subkey_list[6], (RETENTION_HEADS, PROMPT_TOKENS), jnp.float32, 0.5, 0.8))
    return (-baseline_decay_rate * rough_decay * random_wobble + jnp.where(decay_spikes, spike_log_decay, 0.0)).astype(jnp.float32)


def block_levels(rng, dims, pieces, least, high):
    factor_of, own = 1.0, jax.random.fold_in(rng, 6)
    for position, parts in pieces:
        steps = jnp.exp(jax.random.uniform(jax.random.fold_in(own, position), (parts,), jnp.float32, least / len(pieces), high / len(pieces)))
        factor_of = factor_of * jnp.repeat(steps, dims[position] // parts).reshape([-1 if axis == position else 1 for axis in range(len(dims))])
    return factor_of


def assign_block(key, own, number, rows, count, top, most, lean):
    ranking = jax.random.permutation(key, count)
    packed, ordinary = portions_of(count, rows * top, most, lean, True), portions_of(count, rows * top, most, lean, False)
    places = jnp.arange(count)

    def named(lengths, turn):
        used = int((lengths > 0).sum())
        fixed = max(1, used // 4)
        shifted = fixed + (places - fixed + turn * (used - fixed)) % max(1, count - fixed)
        return jnp.zeros((count,), jnp.int32).at[ranking[jnp.where(places < fixed, places, shifted)]].set(jnp.asarray(lengths, jnp.int32))

    lengths = jnp.where(number % 4 == 0, named(packed, number // 4), named(ordinary, number - number // 4 - 1))
    mixed = jax.random.permutation(jax.random.fold_in(own, 3), count)
    giver, taker = mixed[0:count // 2 * 2:2], mixed[1:count // 2 * 2:2]
    slack = jnp.minimum(lengths[giver] - 1, most - lengths[taker]) // 2
    slack = jnp.where((giver == ranking[0]) | (taker == ranking[0]) | (lengths[taker] == 0), 0, jnp.maximum(slack, 0))
    shifted = jax.random.randint(jax.random.fold_in(own, 4), (count // 2,), 0, 1 << 20) % (slack + 1)
    lengths = lengths.at[giver].add(-shifted).at[taker].add(shifted)
    members = jnp.searchsorted(jnp.cumsum(lengths), jnp.arange(rows * top), side="right").astype(jnp.int32)
    table = members.reshape(top, rows).T
    table = table[jax.random.permutation(jax.random.fold_in(own, 1), rows)]
    turn = jax.random.randint(jax.random.fold_in(own, 2), (rows, 1), 0, top)
    return jnp.take_along_axis(table, (jnp.arange(top)[None, :] + turn) % top, axis=1)


def portions_of(count, total, reach, skew, full):
    loads = [(1 << 20) // math.isqrt(rank ** skew) + 1 for rank in range(1, count + 1)]
    largest = reach if full else min(reach, max(-(-total // count), total * loads[0] // sum(loads)))
    least = 1 if total - largest >= count - 1 else 0
    holding, surplus = [largest] + [least] * (count - 1), total - largest - least * (count - 1)
    while surplus > 0:
        free = [i for i in range(1, count) if holding[i] < largest] or [i for i in range(1, count) if holding[i] < reach]
        mass, remaining = sum([loads[i] for i in free]), surplus
        for i in free:
            more = min(reach - holding[i], max(1, remaining * loads[i] // mass), surplus)
            holding[i] = holding[i] + more
            surplus = surplus - more
    return np.array(holding)


def bell_draw(rng, extent, deviation, limit, pieces=(), held_as=jnp.bfloat16):
    loudness = block_levels(rng, extent, pieces, -0.22, 0.18) if pieces else 1.0
    values = jax.random.normal(rng, extent, jnp.float32) * deviation * loudness
    return jnp.minimum(jnp.maximum(values, -limit), limit).astype(held_as)


def setup_inputs(seed: int = 0) -> dict:
    streams_of = jax.random.split(jax.random.key(seed), 11)
    q_prompt = bell_draw(streams_of[0], (PROMPT_TOKENS, RETENTION_HEADS, HD), 0.0625, 0.3984375, ((0, 16), (1, 8)))
    k_prompt = bell_draw(streams_of[1], (PROMPT_TOKENS, RETENTION_HEADS, HD), 0.0625, 0.3984375, ((0, 16), (1, 8)))
    v_prompt = bell_draw(streams_of[2], (PROMPT_TOKENS, RETENTION_HEADS, HD), 1.0, 6.0, ((0, 16), (1, 8)))
    log_decay = draw_log_decay(jax.random.fold_in(streams_of[10], 71), 0)
    prompt_section_keys = jax.random.split(jax.random.fold_in(streams_of[4], 1), ROWS // ROWS_DEV)
    prompt_section_turns = jax.random.permutation(jax.random.fold_in(streams_of[4], 3), ROWS // ROWS_DEV)
    prompt_section = jax.vmap(lambda own, number: assign_block(jax.random.fold_in(streams_of[4], 2), own, number, ROWS_DEV, N_CTX, 1, CAP, 1))(prompt_section_keys, prompt_section_turns).reshape((ROWS, 1))
    q_step = bell_draw(streams_of[5], (ROWS, STEPS, RETENTION_HEADS, HD), 0.0625, 0.3984375, ((0, 16), (2, 8)))
    k_step = bell_draw(streams_of[6], (ROWS, STEPS, RETENTION_HEADS, HD), 0.5, 3.0, ((0, 16), (2, 8)))
    v_step = bell_draw(streams_of[7], (ROWS, STEPS, RETENTION_HEADS, HD), 1.0, 6.0, ((0, 16), (2, 8)))
    step_decay = jnp.clip(-0.6 + 0.55 * jax.random.uniform(streams_of[8], (RETENTION_HEADS, STEPS, ROWS), jnp.float32) ** block_levels(streams_of[8], (RETENTION_HEADS, STEPS, ROWS), ((0, 8), (2, 16)), -0.2, 0.2), -0.6, -0.05)
    w_out = bell_draw(streams_of[9], (RETENTION_HEADS * HD, D), (RETENTION_HEADS * HD) ** -0.5, 0.0625, ((1, 8),))
    return {"q_prompt": q_prompt, "k_prompt": k_prompt, "v_prompt": v_prompt, "log_decay": log_decay, "prompt_section": prompt_section, "q_step": q_step, "k_step": k_step, "v_step": v_step, "step_decay": step_decay, "w_out": w_out}


def block_step(carry_state, block_pair):
    query_rows, key_matrix_rows, value_rows, log_rates = block_pair
    positions = jnp.arange(BLOCK)
    causal = positions[:, None] >= positions[None, :]
    cumlog = jnp.cumsum(log_rates, axis=1)
    decays = jnp.where(causal[None], jnp.exp(jnp.minimum(cumlog[:, :, None] - cumlog[:, None, :], 0.0)), 0.0)
    attention_scores = jnp.einsum('jsv,csv->sjc', query_rows.astype(jnp.float32), key_matrix_rows.astype(jnp.float32))
    weights = (attention_scores * decays).astype(jnp.bfloat16)
    within = jnp.einsum('hnm,mhe->nhe', weights.astype(jnp.float32), value_rows.astype(jnp.float32))
    carried = jnp.einsum('nhd,hde->nhe', query_rows.astype(jnp.float32), carry_state, precision=lax.Precision.HIGHEST)
    carried = carried * jnp.exp(cumlog).T[:, :, None]
    last_log = cumlog[:, -1]
    weighted_values = (key_matrix_rows.astype(jnp.float32) * jnp.exp(last_log[:, None] - cumlog).T[:, :, None]).astype(jnp.bfloat16)
    state_update = jnp.einsum('jxa,jxp->xap', weighted_values.astype(jnp.float32), value_rows.astype(jnp.float32))
    carry_state = jnp.exp(last_log)[:, None, None] * carry_state + state_update
    return carry_state, (within + carried).astype(jnp.bfloat16)


def section_step(carry_state, section_pair):
    carry_state, retained = lax.scan(block_step, carry_state, section_pair)
    return carry_state, (retained, carry_state)


def reference(q_prompt, k_prompt, v_prompt, log_decay, prompt_section, q_step, k_step, v_step, step_decay, w_out):
    block_count = TOK_DEV // BLOCK

    def reshaped(array):
        return array.reshape(N_CTX, block_count, BLOCK, RETENTION_HEADS, HD)

    log_blocks = log_decay.reshape(RETENTION_HEADS, N_CTX, block_count, BLOCK).transpose(1, 2, 0, 3)
    zero_state = jnp.zeros((RETENTION_HEADS, HD, HD), jnp.float32)
    ignored, (retained, boundaries) = lax.scan(
        section_step, zero_state, (reshaped(q_prompt), reshaped(k_prompt), reshaped(v_prompt), log_blocks))
    retention = retained.reshape(PROMPT_TOKENS, RETENTION_HEADS * HD)
    prompt_out = jnp.dot(retention, w_out, preferred_element_type=jnp.float32).astype(jnp.bfloat16)

    section_ids = prompt_section[:, 0]
    step_queries = q_step.astype(jnp.float32)

    def read_one(running, section_pair):
        section_index, boundary = section_pair
        selector = (section_ids == section_index).astype(jnp.float32)
        reads = jnp.einsum('rthd,hde->rthe', step_queries, boundary, precision=lax.Precision.HIGHEST)
        return running + selector[:, None, None, None] * reads, None

    prefix_reads, ignored_too = lax.scan(
        read_one, jnp.zeros((ROWS, STEPS, RETENTION_HEADS, HD), jnp.float32),
        (jnp.arange(N_CTX, dtype=jnp.int32), boundaries))
    step_logs = jnp.cumsum(jnp.transpose(step_decay, (2, 1, 0)), axis=1)
    head_logs = jnp.transpose(step_logs, (0, 2, 1))
    step_index = jnp.arange(STEPS)
    causal = step_index[:, None] >= step_index[None, :]
    step_weights = jnp.where(causal[None, None], jnp.exp(jnp.minimum(head_logs[:, :, :, None] - head_logs[:, :, None, :], 0.0)), 0.0)
    attention_scores = jnp.einsum('rthd,ruhd->rhtu', step_queries, k_step.astype(jnp.float32))
    own_terms = jnp.einsum('rhtu,ruhe->rthe', attention_scores * step_weights, v_step.astype(jnp.float32))
    step_retention = (jnp.exp(step_logs)[:, :, :, None] * prefix_reads + own_terms).astype(jnp.bfloat16)
    step_flat = step_retention.reshape(ROWS * STEPS, RETENTION_HEADS * HD)
    step_out = jnp.dot(step_flat, w_out, preferred_element_type=jnp.float32).astype(jnp.bfloat16)
    return prompt_out, step_out.reshape(ROWS, STEPS, D)
```

```python
import jax
import jax.numpy as jnp
from jax import lax
from jax.experimental import pallas as pl
from jax.experimental.pallas import tpu as pltpu
from jax.sharding import PartitionSpec as P

CAP = 4
BF, F32 = jnp.bfloat16, jnp.float32


def up(a):
    return lax.ppermute(a, "head", [(h, (h + 2) % 8) for h in range(8)])


def down(a):
    return lax.ppermute(a, "head", [(h, (h - 2) % 8) for h in range(8)])


def across(a):
    return lax.ppermute(a, "head", [(h, h ^ 1) for h in range(8)])


def three_parts(value):
    high = value.astype(BF)
    rest = value - lax.optimization_barrier(high).astype(F32)
    middle = rest.astype(BF)
    low = (rest - lax.optimization_barrier(middle).astype(F32)).astype(BF)
    return high, middle, low


def project(accs, srcs, terms, heads, w, final):
    width, tile = srcs[0].shape[1], 256
    old = [a for a in accs if not isinstance(a, int)]
    rows = [a if isinstance(a, int) else a.shape[0] for a in accs]
    n_slot = len(heads)

    def body(heads_ref, *refs):
        src_refs, refs = refs[: len(srcs)], refs[len(srcs) :]
        w_refs, refs = refs[:n_slot], refs[n_slot:]
        old_refs, out_refs = list(refs[: len(old)]), refs[len(old) :]
        for k, acc in enumerate(accs):
            start = None if isinstance(acc, int) else old_refs.pop(0)
            spans = sorted({(t[5], t[3]) for t in terms if t[4] == k})
            for a0, n in spans:
                total = None if start is None else start[a0 : a0 + n, :]
                for slot, i, s0, m, kk, b0 in terms:
                    if kk == k and b0 == a0:
                        part = jnp.dot(
                            src_refs[i][s0 : s0 + m, :],
                            w_refs[slot][...],
                            preferred_element_type=F32,
                        )
                        total = part if total is None else total + part
                out_refs[k][a0 : a0 + n, :] = total.astype(out_refs[k].dtype)

    def w_spec(slot):
        return pl.BlockSpec((width, tile), lambda j, heads_ref, slot=slot: (heads_ref[slot], j))

    columns = w.shape[1]
    flops = sum(2 * t[3] * width * columns for t in terms)
    out = pl.pallas_call(
        body,
        grid_spec=pltpu.PrefetchScalarGridSpec(
            num_scalar_prefetch=1,
            grid=(columns // tile,),
            in_specs=[pl.BlockSpec(s.shape, lambda j, h: (0, 0)) for s in srcs]
            + [w_spec(slot) for slot in range(n_slot)]
            + [pl.BlockSpec((a.shape[0], tile), lambda j, h: (0, j)) for a in old],
            out_specs=[pl.BlockSpec((r, tile), lambda j, h: (0, j)) for r in rows],
        ),
        out_shape=[
            jax.ShapeDtypeStruct((r, columns), BF if f else F32) for r, f in zip(rows, final)
        ],
        compiler_params=pltpu.CompilerParams(vmem_limit_bytes=40 << 20),
        cost_estimate=pl.CostEstimate(
            flops=flops, bytes_accessed=2 * n_slot * width * columns, transcendentals=0
        ),
    )(jnp.stack(heads).astype(jnp.int32), *srcs, *([w] * n_slot), *old)
    return out


def gathered_projections(retention, steps_of, w_out):
    me = lax.axis_index("head")
    z, x = me // 2, me % 2
    here, far = lambda d: ((z + d) % 4) * 2 + x, lambda d: ((z + d) % 4) * 2 + 1 - x
    cat = lambda *parts: jnp.concatenate(parts, axis=0)
    h = retention.shape[0] // 2
    a1, a2, a3 = up(retention), down(retention), across(retention)
    (pa,) = project([2 * h], [retention], [(0, 0, 0, 2 * h, 0, 0)], [me], w_out, [False])
    steps = steps_of()
    r, q = steps.shape[0], steps.shape[0] // 2
    u2 = up(cat(a1[:h], a3[:h], steps))
    d2 = down(cat(a2[h:], a3[:h], steps))
    x2 = across(cat(a1[h:], a2[h:], steps))
    pa, pb = project(
        [pa, r],
        [a1, a2, a3, steps],
        [(s, s, 0, 2 * h, 0, 0) for s in range(3)] + [(3, 3, 0, r, 1, 0)],
        [here(-1), here(1), far(0), me],
        w_out,
        [False, False],
    )
    e = 2 * h
    u3 = up(cat(u2[h:e], u2[e : e + q], x2[e : e + q]))
    d3 = down(cat(x2[h:e], d2[e + q :], x2[e : e + q]))
    x3 = across(cat(u2[e + q :], d2[e + q :]))
    pa, pb = project(
        [pa, pb],
        [u2, d2, x2],
        [
            (0, 0, 0, h, 0, 0),
            (0, 1, 0, h, 0, h),
            (1, 0, h, h, 0, 0),
            (1, 2, 0, h, 0, h),
            (2, 1, h, h, 0, 0),
            (2, 2, h, h, 0, h),
            (3, 0, e, r, 1, 0),
            (4, 1, e, r, 1, 0),
            (5, 2, e, r, 1, 0),
        ],
        [here(2), far(-1), far(1), here(-1), here(1), far(0)],
        w_out,
        [False, False],
    )
    u4, d4 = up(u3[h + q :]), down(x3[q:])
    prompt_out, pb = project(
        [pa, pb],
        [u3, d3, x3],
        [
            (0, 0, 0, h, 0, 0),
            (0, 1, 0, h, 0, h),
            (1, 0, h, q, 1, 0),
            (1, 1, h, q, 1, q),
            (2, 0, h + q, q, 1, 0),
            (2, 2, 0, q, 1, q),
            (3, 1, h + q, q, 1, 0),
            (3, 2, q, q, 1, q),
        ],
        [far(2), here(2), far(-1), far(1)],
        w_out,
        [True, False],
    )
    (step_out,) = project(
        [pb], [u4, d4], [(0, 0, 0, q, 0, 0), (0, 1, 0, q, 0, q)], [far(2)], w_out, [True]
    )
    return prompt_out, step_out


def shards(
    q_prompt,
    k_prompt,
    v_prompt,
    log_decay,
    prompt_section,
    q_step,
    k_step,
    v_step,
    step_decay,
    w_out,
):
    tokens, heads, dim = q_prompt.shape
    sections = lax.axis_size("ctx")
    mine = lax.axis_index("ctx")
    rows, steps = q_step.shape[:2]

    at = jnp.arange(tokens)
    upto = (at[:, None] <= at[None, :]).astype(F32)
    cumlog = jnp.dot(log_decay, upto, precision=lax.Precision.HIGHEST)
    last_log = cumlog[:, -1]
    keys = (k_prompt.astype(F32) * jnp.exp(last_log[:, None] - cumlog).T[:, :, None]).astype(BF)
    own_state = jnp.einsum("jxa,jxp->xap", keys, v_prompt, preferred_element_type=F32)
    total_decay = jnp.exp(last_log)

    ids = prompt_section[:, 0]
    hot = (ids[:, None] == jnp.arange(sections)[None, :]).astype(F32)
    before = jnp.tril(jnp.ones((rows, rows), F32), -1)
    ranking = jnp.sum(jnp.dot(before, hot) * hot, axis=1).astype(jnp.int32)
    slots = ids * CAP + ranking
    selector = (jnp.arange(sections * CAP)[:, None] == slots[None, :]).astype(BF)
    packed = jnp.dot(selector, q_step.reshape(rows, -1), preferred_element_type=F32).astype(BF)
    packed = packed.reshape(sections, CAP * steps * heads, dim)

    slice_rows = heads * dim // sections
    per_head = sections // heads
    parts = jnp.stack(three_parts(total_decay), axis=1)
    parts = jnp.broadcast_to(parts[:, None, :, None], (heads, per_head, 3, dim))
    parts = jnp.pad(parts.reshape(sections, 3, dim), ((0, 0), (0, 13), (0, 0)))
    sent = jnp.concatenate(
        [own_state.astype(BF).reshape(sections, slice_rows, dim), packed, parts], axis=1
    )
    got = lax.all_to_all(sent, "ctx", 0, 0)
    pieces = got[:, :slice_rows].astype(F32)
    queries = got[:, slice_rows : 2 * slice_rows]
    factor = got[:, 2 * slice_rows : 2 * slice_rows + 3, :1].astype(F32)
    factor = factor[:, 0] + factor[:, 1] + factor[:, 2]
    state = jnp.zeros((slice_rows, dim), F32)
    entries = []
    for c in range(sections):
        entries.append(state.astype(BF))
        state = factor[c] * state + pieces[c]
    entry = lax.all_to_all(jnp.stack(entries), "ctx", 0, 0).reshape(heads, dim, dim)

    causal = at[:, None] >= at[None, :]
    decays = jnp.where(
        causal[None], jnp.exp(jnp.minimum(cumlog[:, :, None] - cumlog[:, None, :], 0.0)), 0.0
    )
    scores = jnp.einsum("jsv,csv->sjc", q_prompt, k_prompt, preferred_element_type=F32)
    weights = (scores * decays).astype(BF)
    within = jnp.einsum("hnm,mhe->nhe", weights, v_prompt, preferred_element_type=F32)
    carried = jnp.einsum("nhd,hde->nhe", q_prompt, entry, preferred_element_type=F32)
    retention = (within + carried * jnp.exp(cumlog).T[:, :, None]).astype(BF)
    retention = retention.reshape(tokens, heads * dim)

    def steps_of():
        final = (total_decay[:, None, None] * entry.astype(F32) + own_state).astype(BF)
        asked = queries.reshape(sections, CAP * steps, heads, dim)
        reads = jnp.einsum("jchd,hde->jche", asked, final, preferred_element_type=F32)
        reads = lax.all_to_all(reads.astype(BF).reshape(sections, -1, dim), "ctx", 0, 0)
        reads = reads.reshape(sections * CAP, steps * heads * dim)
        prefix = jnp.dot(selector.T, reads, preferred_element_type=F32)
        prefix = prefix.reshape(rows, steps, heads, dim)
        rates = jnp.transpose(step_decay, (2, 1, 0))
        logs = [rates[:, 0]]
        for t in range(1, steps):
            logs.append(logs[-1] + rates[:, t])
        step_logs = jnp.stack(logs, axis=1)
        head_logs = jnp.transpose(step_logs, (0, 2, 1))
        turn = jnp.arange(steps)
        seen = turn[:, None] >= turn[None, :]
        gaps = head_logs[:, :, :, None] - head_logs[:, :, None, :]
        gains = jnp.where(seen[None, None], jnp.exp(jnp.minimum(gaps, 0.0)), 0.0)
        own = jnp.einsum("rthd,ruhd->rhtu", q_step, k_step, preferred_element_type=F32)
        own = jnp.einsum("rhtu,ruhe->rthe", own * gains, v_step.astype(F32))
        kept = (jnp.exp(step_logs)[:, :, :, None] * prefix + own).astype(BF)
        return kept.reshape(rows * steps, heads * dim)

    prompt_out, step_out = gathered_projections(retention, steps_of, w_out)
    return prompt_out, step_out.reshape(rows, steps, w_out.shape[1])


def solution(mesh):
    in_specs = (
        P("ctx", "head", None),
        P("ctx", "head", None),
        P("ctx", "head", None),
        P("head", "ctx"),
        P("ctx", None),
        P("ctx", None, "head", None),
        P("ctx", None, "head", None),
        P("ctx", None, "head", None),
        P("head", None, "ctx"),
        P(None, "head"),
    )
    out_specs = (P("ctx", "head"), P("ctx", None, "head"))
    return jax.shard_map(shards, mesh=mesh, in_specs=in_specs, out_specs=out_specs, check_vma=False)
```

```python
import jax
import jax.numpy as jnp
from jax import lax
from jax.experimental import pallas as pl
from jax.experimental.pallas import tpu as pltpu
from jax.sharding import PartitionSpec as P

CAP = 4
BF, F32 = jnp.bfloat16, jnp.float32
WHOLE = pl.BlockSpec(memory_space=pltpu.VMEM)


def up(a):
    return lax.ppermute(a, "head", [(h, (h + 2) % 8) for h in range(8)])


def down(a):
    return lax.ppermute(a, "head", [(h, (h - 2) % 8) for h in range(8)])


def across(a):
    return lax.ppermute(a, "head", [(h, h ^ 1) for h in range(8)])


def after(values, *others):
    return lax.optimization_barrier((values, others))[0]


def call(body, out, ins, flops, limit=6 << 20):
    size = sum(a.size * a.dtype.itemsize for a in (*ins, *out))
    return pl.pallas_call(
        body,
        in_specs=[WHOLE] * len(ins),
        out_specs=[WHOLE] * len(out),
        out_shape=list(out),
        compiler_params=pltpu.CompilerParams(vmem_limit_bytes=limit),
        cost_estimate=pl.CostEstimate(flops=flops, bytes_accessed=size, transcendentals=0),
    )(*ins)


def project(accs, srcs, terms, heads, w, final):
    width, tile = srcs[0].shape[1], 256
    columns = w.shape[1]
    old = [a for a in accs if not isinstance(a, int)]
    rows = [a if isinstance(a, int) else a.shape[0] for a in accs]

    n_slot = len(heads)

    def body(heads_ref, *refs):
        src_refs, refs = refs[: len(srcs)], refs[len(srcs) :]
        w_ref, refs = refs[0], refs[1:]
        old_refs, out_refs = list(refs[: len(old)]), refs[len(old) : len(old) + len(accs)]
        sums, (w_held, arrived) = refs[len(old) + len(accs) : -2], refs[-2:]
        copies = []
        for slot in range(n_slot):
            first = pl.multiple_of(heads_ref[slot] * width, width)
            copies.append(
                pltpu.make_async_copy(
                    w_ref.at[pl.ds(first, width), :], w_held.at[slot], arrived.at[slot]
                )
            )
            copies[-1].start()
        fresh = {}
        for k, acc in enumerate(accs):
            if not isinstance(acc, int):
                fresh[k] = old_refs.pop(0)
        seen = set()
        last = {(t[4], t[5]): t[0] for t in terms}
        for slot in range(n_slot):
            copies[slot].wait()
            mine = [t for t in terms if t[0] == slot]

            @pl.loop(0, columns // tile)
            def _(j, slot=slot, mine=mine, seen=frozenset(seen)):
                cols = pl.ds(pl.multiple_of(j * tile, tile), tile)
                for _, i, s0, m, k, a0 in mine:
                    total = jnp.dot(
                        src_refs[i][s0 : s0 + m, :],
                        w_held[slot, :, cols],
                        preferred_element_type=F32,
                    )
                    span = slice(a0, a0 + m)
                    if (k, a0) in seen:
                        total += sums[k][span, cols]
                    elif k in fresh:
                        total += fresh[k][span, cols]
                    if last[k, a0] == slot:
                        out_refs[k][span, cols] = total.astype(out_refs[k].dtype)
                    else:
                        sums[k][span, cols] = total

            seen |= {(t[4], t[5]) for t in mine}

    flops = sum(2 * t[3] * width * columns for t in terms)
    return pl.pallas_call(
        body,
        in_specs=[pl.BlockSpec(memory_space=pltpu.SMEM)]
        + [WHOLE] * len(srcs)
        + [pl.BlockSpec(memory_space=pltpu.HBM)]
        + [WHOLE] * len(old),
        out_specs=[WHOLE] * len(rows),
        out_shape=[
            jax.ShapeDtypeStruct((r, columns), BF if f else F32) for r, f in zip(rows, final)
        ],
        scratch_shapes=[pltpu.VMEM((r, columns), F32) for r in rows]
        + [
            pltpu.VMEM((n_slot, width, columns), BF),
            pltpu.SemaphoreType.DMA((n_slot,)),
        ],
        compiler_params=pltpu.CompilerParams(vmem_limit_bytes=48 << 20),
        cost_estimate=pl.CostEstimate(
            flops=flops, bytes_accessed=n_slot * 2 * width * columns, transcendentals=0
        ),
    )(jnp.stack(heads).astype(jnp.int32), *srcs, w, *old)


def scan_sections(got, slice_rows):
    sections, _, dim = got.shape

    def body(got_ref, out_ref):
        state = jnp.zeros((slice_rows, dim), F32)
        for c in range(sections):
            out_ref[c] = state.astype(BF)
            parts = got_ref[c, slice_rows : slice_rows + 16, :].astype(F32)
            factor = parts[0:1] + parts[1:2] + parts[2:3]
            state = factor * state + got_ref[c, :slice_rows, :].astype(F32)

    shape = jax.ShapeDtypeStruct((sections, slice_rows, dim), BF)
    return call(body, [shape], [got], sections * slice_rows * dim * 4)[0]


def read_states(queries, within, gains, entry, own_state, decay, asked):
    heads, dim, _ = entry.shape

    def body(q_ref, in_ref, g_ref, e_ref, s_ref, d_ref, a_ref, r_ref, o_ref):
        for h in range(heads):
            cols = slice(h * dim, (h + 1) * dim)
            state = e_ref[h]
            last = (d_ref[0, h] * state.astype(F32) + s_ref[h]).astype(BF)
            rows = a_ref[:, h].reshape(-1, dim)
            reads = jnp.dot(rows, last, preferred_element_type=F32)
            o_ref[:, h] = reads.astype(BF).reshape(a_ref.shape[0], -1, dim)
            carried = jnp.dot(q_ref[:, cols], state, preferred_element_type=F32)
            total = in_ref[:, cols] + g_ref[:, h : h + 1] * carried
            r_ref[:, cols] = total.astype(BF)

    specs = [WHOLE] * 7
    specs[5] = pl.BlockSpec(memory_space=pltpu.SMEM)
    return pl.pallas_call(
        body,
        in_specs=specs,
        out_specs=[WHOLE] * 2,
        out_shape=[
            jax.ShapeDtypeStruct(queries.shape, BF),
            jax.ShapeDtypeStruct(asked.shape, BF),
        ],
        compiler_params=pltpu.CompilerParams(vmem_limit_bytes=8 << 20),
        cost_estimate=pl.CostEstimate(
            flops=2 * 768 * heads * dim * dim, bytes_accessed=8 << 20, transcendentals=0
        ),
    )(queries, within, gains, entry, own_state, decay, asked)


def pack_queries(selector, queries, sections, heads):
    dim = queries.shape[1] // heads

    def body(s_ref, q_ref, o_ref):
        for h in range(heads):
            picked = jnp.dot(
                s_ref[...], q_ref[:, h * dim : (h + 1) * dim], preferred_element_type=F32
            )
            o_ref[:, h] = picked.astype(BF).reshape(sections, -1, dim)

    slots = selector.shape[0] // sections
    shape = jax.ShapeDtypeStruct((sections, heads, slots, dim), BF)
    return call(body, [shape], [selector, queries], 2 * selector.size * queries.shape[1])[0]


def finish_steps(selector, reads, gains, own):
    _, heads, _, dim = reads.shape

    def body(s_ref, r_ref, g_ref, own_ref, o_ref):
        for h in range(heads):
            cols = slice(h * dim, (h + 1) * dim)
            prefix = jnp.dot(
                s_ref[...], r_ref[:, h].reshape(-1, dim), preferred_element_type=F32
            )
            o_ref[:, cols] = (g_ref[:, h : h + 1] * prefix + own_ref[:, cols]).astype(BF)

    shape = jax.ShapeDtypeStruct(own.shape, BF)
    return call(body, [shape], [selector, reads, gains, own], 2 * selector.size * own.shape[1])[0]


def gathered_projections(retention, steps_of, w):
    me = lax.axis_index("head")
    z, x = me // 2, me % 2
    here, far = lambda d: ((z + d) % 4) * 2 + x, lambda d: ((z + d) % 4) * 2 + 1 - x
    n = retention.shape[0]
    third = n * 11 // 32

    a1, a2, a3 = up(retention), down(retention), across(retention)
    (pa,) = project([n], [retention], [(0, 0, 0, n, 0, 0)], [me], w, [False])
    a1, a2, a3, pa = lax.optimization_barrier((a1, a2, a3, pa))

    b1, b2, b3 = up(a3), down(a2), across(a2)
    steps = steps_of(a1)
    r = steps.shape[0]
    c1, c2, c3 = up(steps), down(steps), across(steps)
    (pa,) = project(
        [pa],
        [a1, a2, a3],
        [(s, s, 0, n, 0, 0) for s in range(3)],
        [here(-1), here(1), far(0)],
        w,
        [False],
    )
    b1, b2, b3, c1, c2, c3, pa = lax.optimization_barrier((b1, b2, b3, c1, c2, c3, pa))

    e1, e2, e3 = up(b1[:third]), down(b3[third : 2 * third]), across(b2[2 * third :])
    d1, d2, d3 = up(c3), down(c2), across(c2)
    pa, pb = project(
        [pa, r],
        [b1, b2, b3, steps, c1, c2, c3],
        [(s, s, 0, n, 0, 0) for s in range(3)] + [(3 + s, 3 + s, 0, r, 1, 0) for s in range(4)],
        [far(-1), here(2), far(1), me, here(-1), here(1), far(0)],
        w,
        [False, False],
    )
    e1, e2, e3, d1, d2, d3, pa, pb = lax.optimization_barrier((e1, e2, e3, d1, d2, d3, pa, pb))

    f1, f2 = up(d1[: r // 2]), down(d3[r // 2 :])
    prompt_out, pb = project(
        [pa, pb],
        [e1, e2, e3, d1, d2, d3],
        [
            (0, 0, 0, third, 0, 0),
            (0, 1, 0, third, 0, third),
            (0, 2, 0, n - 2 * third, 0, 2 * third),
        ]
        + [(1 + s, 3 + s, 0, r, 1, 0) for s in range(3)],
        [far(2), far(-1), here(2), far(1)],
        w,
        [True, False],
    )
    f1, f2, pb = lax.optimization_barrier((f1, f2, pb))
    (step_out,) = project(
        [pb],
        [f1, f2],
        [(0, 0, 0, r // 2, 0, 0), (0, 1, 0, r // 2, 0, r // 2)],
        [far(2)],
        w,
        [True],
    )
    return prompt_out, step_out


def shards(
    q_prompt,
    k_prompt,
    v_prompt,
    log_decay,
    prompt_section,
    q_step,
    k_step,
    v_step,
    step_decay,
    w_out,
):
    tokens, heads, dim = q_prompt.shape
    sections = lax.axis_size("ctx")
    rows, steps = q_step.shape[:2]

    at = jnp.arange(tokens)
    upto = (at[:, None] <= at[None, :]).astype(F32)
    cumlog = jnp.dot(log_decay, upto, precision=lax.Precision.HIGHEST)
    last_log = cumlog[:, -1]
    keys = (k_prompt.astype(F32) * jnp.exp(last_log[:, None] - cumlog).T[:, :, None]).astype(BF)
    own_state = jnp.einsum("jxa,jxp->xap", keys, v_prompt, preferred_element_type=F32)
    total_decay = jnp.exp(last_log)
    slice_rows = heads * dim // sections
    high = lax.reduce_precision(total_decay, 8, 7)
    middle = lax.reduce_precision(total_decay - high, 8, 7)
    parts = jnp.stack([high, middle, total_decay - high - middle], axis=1).astype(BF)
    parts = jnp.broadcast_to(parts[:, None, :, None], (heads, sections // heads, 3, dim))
    parts = jnp.pad(parts.reshape(sections, 3, dim), ((0, 0), (0, 13), (0, 0)))
    sent = jnp.concatenate([own_state.astype(BF).reshape(sections, slice_rows, dim), parts], axis=1)
    got = lax.all_to_all(sent, "ctx", 0, 0)

    q_step, prompt_section = after((q_step, prompt_section), sent)
    ids = prompt_section[:, 0]
    hot = (ids[:, None] == jnp.arange(sections)[None, :]).astype(F32)
    before = jnp.tril(jnp.ones((rows, rows), F32), -1)
    ranking = jnp.sum(jnp.dot(before, hot) * hot, axis=1).astype(jnp.int32)
    slots = (ids * CAP + ranking)[:, None] * steps + jnp.arange(steps)[None, :]
    slots = slots.reshape(rows * steps)
    every = jnp.arange(sections * CAP * steps)
    selector = (slots[:, None] == every[None, :]).astype(BF)
    flipped = (every[:, None] == slots[None, :]).astype(BF)
    packed = pack_queries(flipped, q_step.reshape(rows * steps, -1), sections, heads)
    asked = lax.all_to_all(packed, "ctx", 0, 0)

    q_late, k_late, v_late, cum_late = after((q_prompt, k_prompt, v_prompt, cumlog), packed)
    causal = at[:, None] >= at[None, :]
    decays = jnp.where(
        causal[None], jnp.exp(jnp.minimum(cum_late[:, :, None] - cum_late[:, None, :], 0.0)), 0.0
    )
    scores = jnp.einsum("jsv,csv->sjc", q_late, k_late, preferred_element_type=F32)
    weights = (scores * decays).astype(BF)
    within = jnp.einsum("hnm,mhe->nhe", weights, v_late, preferred_element_type=F32)
    within = within.reshape(tokens, heads * dim)
    queries = q_late.reshape(tokens, heads * dim)
    gains = jnp.exp(cum_late).T

    entries = scan_sections(got, slice_rows)
    entry = lax.all_to_all(entries, "ctx", 0, 0).reshape(heads, dim, dim)

    q_own, k_own, v_own, rates = after((q_step, k_step, v_step, step_decay), entries)
    rates = jnp.transpose(rates, (2, 1, 0))
    logs = [rates[:, 0]]
    for t in range(1, steps):
        logs.append(logs[-1] + rates[:, t])
    step_logs = jnp.stack(logs, axis=1)
    head_logs = jnp.transpose(step_logs, (0, 2, 1))
    turn = jnp.arange(steps)
    seen = turn[:, None] >= turn[None, :]
    gaps = head_logs[:, :, :, None] - head_logs[:, :, None, :]
    step_gains = jnp.where(seen[None, None], jnp.exp(jnp.minimum(gaps, 0.0)), 0.0)
    own = jnp.einsum("rthd,ruhd->rhtu", q_own, k_own, preferred_element_type=F32)
    own = jnp.einsum("rhtu,ruhe->rthe", own * step_gains, v_own.astype(F32))
    own = own.reshape(rows * steps, heads * dim)
    kept = jnp.exp(step_logs).reshape(rows * steps, heads)

    within, queries, gains, own, kept, entry, asked = lax.optimization_barrier(
        (within, queries, gains, own, kept, entry, asked)
    )
    retention, reads = read_states(
        queries, within, gains, entry, own_state, total_decay[None, :], asked
    )
    reads = lax.all_to_all(reads, "ctx", 0, 0)

    def steps_of(ready):
        return finish_steps(selector, after(reads, ready), kept, own)

    prompt_out, step_out = gathered_projections(retention, steps_of, w_out)
    return prompt_out, step_out.reshape(rows, steps, w_out.shape[1])


def solution(mesh):
    in_specs = (
        P("ctx", "head", None),
        P("ctx", "head", None),
        P("ctx", "head", None),
        P("head", "ctx"),
        P("ctx", None),
        P("ctx", None, "head", None),
        P("ctx", None, "head", None),
        P("ctx", None, "head", None),
        P("head", None, "ctx"),
        P(None, "head"),
    )
    out_specs = (P("ctx", "head"), P("ctx", None, "head"))
    return jax.shard_map(shards, mesh=mesh, in_specs=in_specs, out_specs=out_specs, check_vma=False)
```

```python
import jax
import jax.numpy as jnp
from jax import lax
from jax.experimental import pallas as pl
from jax.experimental.pallas import tpu as pltpu
from jax.sharding import PartitionSpec as P

TILE = 256
BF, F32 = jnp.bfloat16, jnp.float32
WHOLE = pl.BlockSpec(memory_space=pltpu.VMEM)


def up(a):
    return lax.ppermute(a, "head", [(h, (h + 2) % 8) for h in range(8)])


def down(a):
    return lax.ppermute(a, "head", [(h, (h - 2) % 8) for h in range(8)])


def across(a):
    return lax.ppermute(a, "head", [(h, h ^ 1) for h in range(8)])


def after(values, *others):
    return lax.optimization_barrier((values, others))[0]


def call(body, out, ins, flops, limit=6 << 20):
    size = sum(a.size * a.dtype.itemsize for a in (*ins, *out))
    return pl.pallas_call(
        body,
        in_specs=[WHOLE] * len(ins),
        out_specs=[WHOLE] * len(out),
        out_shape=list(out),
        compiler_params=pltpu.CompilerParams(vmem_limit_bytes=limit),
        cost_estimate=pl.CostEstimate(flops=flops, bytes_accessed=size, transcendentals=0),
    )(*ins)


def project(total, srcs, terms, heads, w, split=None):
    width, tile = srcs[0].shape[1], TILE
    columns, n_slot = w.shape[1], len(heads)
    old = [] if isinstance(total, int) else [total]
    rows = total if isinstance(total, int) else total.shape[0]

    def body(heads_ref, *refs):
        src_refs, w_ref, refs = refs[: len(srcs)], refs[len(srcs)], refs[len(srcs) + 1 :]
        old_refs, out_refs, (w_held, arrived) = refs[: len(old)], refs[len(old) : -2], refs[-2:]
        copies = []
        for slot in range(n_slot):
            first = pl.multiple_of(heads_ref[slot] * width, width)
            copies.append(
                pltpu.make_async_copy(
                    w_ref.at[pl.ds(first, width), :], w_held.at[slot], arrived.at[slot]
                )
            )
            copies[-1].start()
        for slot in range(n_slot):
            copies[slot].wait()
            mine = [t for t in terms if t[0] == slot]

            @pl.loop(0, columns // tile)
            def _(j, slot=slot, mine=mine):
                cols = pl.ds(pl.multiple_of(j * tile, tile), tile)
                for _, i, s0, n, a0 in mine:
                    part = jnp.dot(
                        src_refs[i][s0 : s0 + n, :],
                        w_held[slot, :, cols],
                        preferred_element_type=F32,
                    )
                    if slot:
                        part += out_refs[0][a0 : a0 + n, cols]
                    elif old:
                        part += old_refs[0][a0 : a0 + n, cols]
                    if split is None:
                        out_refs[0][a0 : a0 + n, cols] = part
                    else:
                        top = min(max(split - a0, 0), n)
                        if top:
                            out_refs[0][a0 : a0 + top, cols] = part[:top].astype(BF)
                        if top < n:
                            below = a0 + top - split
                            out_refs[1][below : below + n - top, cols] = part[top:].astype(BF)

    if split is None:
        out = [jax.ShapeDtypeStruct((rows, columns), F32)]
    else:
        out = [jax.ShapeDtypeStruct((r, columns), BF) for r in (split, rows - split)]
    flops = sum(2 * t[3] * width * columns for t in terms)
    return pl.pallas_call(
        body,
        in_specs=[pl.BlockSpec(memory_space=pltpu.SMEM)]
        + [WHOLE] * len(srcs)
        + [pl.BlockSpec(memory_space=pltpu.HBM)]
        + [WHOLE] * len(old),
        out_specs=[WHOLE] * len(out),
        out_shape=out,
        scratch_shapes=[
            pltpu.VMEM((n_slot, width, columns), BF),
            pltpu.SemaphoreType.DMA((n_slot,)),
        ],
        compiler_params=pltpu.CompilerParams(vmem_limit_bytes=46 << 20),
        cost_estimate=pl.CostEstimate(
            flops=flops, bytes_accessed=n_slot * 2 * width * columns, transcendentals=0
        ),
    )(jnp.stack(heads).astype(jnp.int32), *srcs, w, *old)


NT = (((1,), (1,)), ((), ()))


def scan_and_read(got, slice_rows, slots):
    sections, _, dim = got.shape
    head_rows, piece = got.shape[1] - slice_rows - slots, slots * slice_rows // dim
    packs = dim // 128

    def body(got_ref, out_ref, ends):
        state = jnp.zeros((slice_rows, dim), F32)
        for c in range(sections):
            out_ref[c, :slice_rows, :] = state.astype(BF)
            header = got_ref[c, slice_rows : slice_rows + 16, :].astype(F32)
            factor = header[0:1] + header[1:2] + header[2:3]
            state = factor * state + got_ref[c, :slice_rows, :].astype(F32)
            ends[c * slice_rows : (c + 1) * slice_rows, :] = state.astype(BF)
        lane = lax.broadcasted_iota(jnp.int32, (slots, 128), 1)
        row = lax.broadcasted_iota(jnp.int32, (slots, 128), 0)
        upper = (lane >= slice_rows).astype(F32)
        low = lax.broadcasted_iota(jnp.int32, (piece, 128), 1) < slice_rows

        @pl.loop(0, sections)
        def _(c):
            asked = got_ref[c, slice_rows + head_rows :, :]
            reads = lax.dot_general(asked, ends[...], NT, preferred_element_type=F32)
            header = got_ref[c, slice_rows : slice_rows + 16, :].astype(F32)
            named = jnp.where(row == lane, header[3:4, :128], 0.0).sum(axis=1, keepdims=True)
            wanted = named - upper
            total = jnp.zeros((slots, 128), F32)
            for j in range(0, sections, 2):
                part = reads[:, j * slice_rows : (j + 2) * slice_rows]
                total += jnp.where(wanted == float(j), part, 0.0)
            total += pltpu.roll(total, slice_rows, 1)
            for p in range(packs):
                first = total[2 * p * piece : (2 * p + 1) * piece]
                second = total[(2 * p + 1) * piece : (2 * p + 2) * piece]
                out_ref[c, slice_rows:, p * 128 : (p + 1) * 128] = jnp.where(
                    low, first, second
                ).astype(BF)

    return pl.pallas_call(
        body,
        in_specs=[WHOLE],
        out_specs=WHOLE,
        out_shape=jax.ShapeDtypeStruct((sections, slice_rows + piece, dim), BF),
        scratch_shapes=[pltpu.VMEM((sections * slice_rows, dim), BF)],
        compiler_params=pltpu.CompilerParams(vmem_limit_bytes=12 << 20),
        cost_estimate=pl.CostEstimate(
            flops=2 * sections * slots * sections * slice_rows * dim,
            bytes_accessed=6 << 20,
            transcendentals=0,
        ),
    )(got)


def retain(queries, within, gains, got, slice_rows, own, kept):
    sections, _, dim = got.shape
    tokens, width = queries.shape
    slots, heads = kept.shape
    per_head = sections // heads
    piece = got.shape[1] - slice_rows

    def body(q_ref, in_ref, g_ref, got_ref, own_ref, k_ref, o_ref):
        low = lax.broadcasted_iota(jnp.int32, (piece, 128), 1) < slice_rows
        for h in range(heads):
            cols = slice(h * dim, (h + 1) * dim)
            state = got_ref[h * per_head : (h + 1) * per_head, :slice_rows, :].reshape(dim, dim)
            carried = lax.dot_general(q_ref[:, cols], state, NT, preferred_element_type=F32)
            total = in_ref[:, cols] + g_ref[:, h : h + 1] * carried
            o_ref[:tokens, cols] = total.astype(BF)
            for b in range(slots // piece):
                rows = slice(b * piece, (b + 1) * piece)
                for p in range(dim // 128):
                    halves = []
                    for side in range(2):
                        held = got_ref[
                            h * per_head + 2 * p + side,
                            slice_rows:,
                            b // 2 * 128 : (b // 2 + 1) * 128,
                        ].astype(F32)
                        halves.append(held if b % 2 == side else pltpu.roll(held, slice_rows, 1))
                    read = jnp.where(low, halves[0], halves[1])
                    at = slice(h * dim + p * 128, h * dim + (p + 1) * 128)
                    mixed = k_ref[rows, h : h + 1] * read + own_ref[rows, at]
                    o_ref[tokens + b * piece : tokens + (b + 1) * piece, at] = mixed.astype(BF)

    out = jax.ShapeDtypeStruct((tokens + slots, width), BF)
    flops = 2 * tokens * width * dim
    return call(body, [out], [queries, within, gains, got, own, kept], flops, 12 << 20)[0]


def gathered_projection(block, split, w):
    me = lax.axis_index("head")
    z, x = me // 2, me % 2
    here, far = lambda d: ((z + d) % 4) * 2 + x, lambda d: ((z + d) % 4) * 2 + 1 - x
    n = block.shape[0]
    third = -(-n // 48) * 16
    whole = lambda s: (s, s, 0, n, 0)

    a1, a2, a3 = up(block), down(block), across(block)
    (total,) = project(n, [block], [whole(0)], [me], w)
    a1, a2, a3, total = lax.optimization_barrier((a1, a2, a3, total))

    b1, b2, b3 = up(a3), down(a2), across(a2)
    (total,) = project(
        total, [a1, a2, a3], [whole(s) for s in range(3)], [here(-1), here(1), far(0)], w
    )
    b1, b2, b3, total = lax.optimization_barrier((b1, b2, b3, total))

    c1, c2, c3 = up(b1[:third]), down(b3[third : 2 * third]), across(b2[2 * third :])
    (total,) = project(
        total, [b1, b2, b3], [whole(s) for s in range(3)], [far(-1), here(2), far(1)], w
    )
    c1, c2, c3, total = lax.optimization_barrier((c1, c2, c3, total))
    return project(
        total,
        [c1, c2, c3],
        [(0, i, 0, c.shape[0], i * third) for i, c in enumerate((c1, c2, c3))],
        [far(2)],
        w,
        split,
    )


def shards(
    q_prompt,
    k_prompt,
    v_prompt,
    log_decay,
    prompt_section,
    q_step,
    k_step,
    v_step,
    step_decay,
    w_out,
):
    tokens, heads, dim = q_prompt.shape
    sections = lax.axis_size("ctx")
    rows, steps = q_step.shape[:2]

    at = jnp.arange(tokens)
    upto = (at[:, None] <= at[None, :]).astype(F32)
    cumlog = jnp.dot(log_decay, upto, precision=lax.Precision.HIGHEST)
    last_log = cumlog[:, -1]
    keys = (k_prompt.astype(F32) * jnp.exp(last_log[:, None] - cumlog).T[:, :, None]).astype(BF)
    own_state = jnp.einsum("jxp,jxa->xpa", v_prompt, keys, preferred_element_type=F32)
    total_decay = jnp.exp(last_log)
    slice_rows, slots = heads * dim // sections, rows * steps
    high = lax.reduce_precision(total_decay, 8, 7)
    middle = lax.reduce_precision(total_decay - high, 8, 7)
    parts = jnp.stack([high, middle, total_decay - high - middle], axis=1).astype(BF)
    parts = jnp.broadcast_to(parts[:, None, :, None], (heads, sections // heads, 3, dim))
    named = jnp.broadcast_to(prompt_section, (rows, steps)).reshape(1, 1, slots).astype(BF)
    named = jnp.pad(named, ((0, 0), (0, 0), (0, dim - slots)))
    named = jnp.broadcast_to(named, (sections, 1, dim))
    header = jnp.concatenate([parts.reshape(sections, 3, dim), named], axis=1)
    header = jnp.pad(header, ((0, 0), (0, 12), (0, 0)))
    asked = q_step.reshape(slots, heads, dim).transpose(1, 0, 2)
    asked = jnp.broadcast_to(asked[:, None], (heads, sections // heads, slots, dim))
    sent = jnp.concatenate(
        [
            own_state.astype(BF).reshape(sections, slice_rows, dim),
            header,
            asked.reshape(sections, slots, dim),
        ],
        axis=1,
    )
    got = lax.all_to_all(sent, "ctx", 0, 0)

    q_late, k_late, v_late, cum_late = after((q_prompt, k_prompt, v_prompt, cumlog), sent)
    causal = at[:, None] >= at[None, :]
    decays = jnp.where(
        causal[None], jnp.exp(jnp.minimum(cum_late[:, :, None] - cum_late[:, None, :], 0.0)), 0.0
    )
    scores = jnp.einsum("jsv,csv->sjc", q_late, k_late, preferred_element_type=F32)
    weights = (scores * decays).astype(BF)
    within = jnp.einsum("hnm,mhe->nhe", weights, v_late, preferred_element_type=F32)
    within = within.reshape(tokens, heads * dim)
    queries = q_late.reshape(tokens, heads * dim)
    gains = jnp.exp(cum_late).T
    got, within, queries, gains = lax.optimization_barrier((got, within, queries, gains))

    sent = scan_and_read(got, slice_rows, slots)
    got = lax.all_to_all(sent, "ctx", 0, 0)

    q_own, k_own, v_own, rates = after((q_step, k_step, v_step, step_decay), sent)
    rates = jnp.transpose(rates, (2, 1, 0))
    logs = [rates[:, 0]]
    for t in range(1, steps):
        logs.append(logs[-1] + rates[:, t])
    step_logs = jnp.stack(logs, axis=1)
    head_logs = jnp.transpose(step_logs, (0, 2, 1))
    turn = jnp.arange(steps)
    seen = turn[:, None] >= turn[None, :]
    gaps = head_logs[:, :, :, None] - head_logs[:, :, None, :]
    step_gains = jnp.where(seen[None, None], jnp.exp(jnp.minimum(gaps, 0.0)), 0.0)
    own = jnp.einsum("rthd,ruhd->rhtu", q_own, k_own, preferred_element_type=F32)
    own = jnp.einsum("rhtu,ruhe->rthe", own * step_gains, v_own.astype(F32))
    own = own.reshape(slots, heads * dim)
    kept = jnp.exp(step_logs).reshape(slots, heads)
    got, own, kept = lax.optimization_barrier((got, own, kept))

    block = retain(queries, within, gains, got, slice_rows, own, kept)
    prompt_out, step_out = gathered_projection(block, tokens, w_out)
    return prompt_out, step_out.reshape(rows, steps, w_out.shape[1])


def solution(mesh):
    in_specs = (
        P("ctx", "head", None),
        P("ctx", "head", None),
        P("ctx", "head", None),
        P("head", "ctx"),
        P("ctx", None),
        P("ctx", None, "head", None),
        P("ctx", None, "head", None),
        P("ctx", None, "head", None),
        P("head", None, "ctx"),
        P(None, "head"),
    )
    out_specs = (P("ctx", "head"), P("ctx", None, "head"))
    return jax.shard_map(shards, mesh=mesh, in_specs=in_specs, out_specs=out_specs, check_vma=False)
```

```python
import jax
import jax.numpy as jnp
from jax import lax
from jax.experimental import pallas as pl
from jax.experimental.pallas import tpu as pltpu
from jax.sharding import PartitionSpec as P

BF, F32 = jnp.bfloat16, jnp.float32
WHOLE = pl.BlockSpec(memory_space=pltpu.VMEM)


def up(a):
    return lax.ppermute(a, "head", [(h, (h + 2) % 8) for h in range(8)])


def down(a):
    return lax.ppermute(a, "head", [(h, (h - 2) % 8) for h in range(8)])


def across(a):
    return lax.ppermute(a, "head", [(h, h ^ 1) for h in range(8)])


def after(values, *others):
    return lax.optimization_barrier((values, others))[0]


def project(total, srcs, terms, heads, w, split=None):
    width, columns = srcs[0].shape[1], w.shape[1]
    n_slot = 0 if heads is None else len(heads)
    old = [] if isinstance(total, int) else [total]
    rows = total if isinstance(total, int) else total.shape[0]

    def add(slot, weights, src_refs, old_refs, out_refs):
        for s, i, s0, n, a0 in terms:
            if s != slot:
                continue
            part = jnp.dot(src_refs[i][s0 : s0 + n, :], weights, preferred_element_type=F32)
            if slot:
                part += out_refs[0][a0 : a0 + n, :]
            elif old:
                part += old_refs[0][a0 : a0 + n, :]
            if split is None:
                out_refs[0][a0 : a0 + n, :] = part
                continue
            top = min(max(split - a0, 0), n)
            if top:
                out_refs[0][a0 : a0 + top, :] = part[:top].astype(BF)
            if top < n:
                below = a0 + top - split
                out_refs[1][below : below + n - top, :] = part[top:].astype(BF)

    def body(*refs):
        if heads is None:
            src_refs, w_ref, refs = refs[: len(srcs)], refs[len(srcs)], refs[len(srcs) + 1 :]
            add(0, w_ref[...], src_refs, refs[: len(old)], refs[len(old) :])
            return
        heads_ref, *refs = refs
        src_refs, w_ref, refs = refs[: len(srcs)], refs[len(srcs)], refs[len(srcs) + 1 :]
        w_held, arrived = refs[-2:]
        copies = []
        for slot in range(n_slot):
            first = pl.multiple_of(heads_ref[slot] * width, width)
            copies.append(
                pltpu.make_async_copy(
                    w_ref.at[pl.ds(first, width), :], w_held.at[slot], arrived.at[slot]
                )
            )
            copies[-1].start()
        for slot in range(n_slot):
            copies[slot].wait()
            add(slot, w_held[slot], src_refs, refs[: len(old)], refs[len(old) : -2])

    if split is None:
        out = [jax.ShapeDtypeStruct((rows, columns), F32)]
    else:
        out = [jax.ShapeDtypeStruct((r, columns), BF) for r in (split, rows - split)]
    flops = sum(2 * t[3] * width * columns for t in terms)
    cost = pl.CostEstimate(
        flops=flops, bytes_accessed=max(n_slot, 1) * 2 * width * columns, transcendentals=0
    )
    if heads is None:
        return pl.pallas_call(
            body,
            in_specs=[WHOLE] * (len(srcs) + 1 + len(old)),
            out_specs=[WHOLE] * len(out),
            out_shape=out,
            compiler_params=pltpu.CompilerParams(vmem_limit_bytes=16 << 20),
            cost_estimate=cost,
        )(*srcs, w, *old)
    return pl.pallas_call(
        body,
        in_specs=[pl.BlockSpec(memory_space=pltpu.SMEM)]
        + [WHOLE] * len(srcs)
        + [pl.BlockSpec(memory_space=pltpu.HBM)]
        + [WHOLE] * len(old),
        out_specs=[WHOLE] * len(out),
        out_shape=out,
        scratch_shapes=[
            pltpu.VMEM((n_slot, width, columns), BF),
            pltpu.SemaphoreType.DMA((n_slot,)),
        ],
        compiler_params=pltpu.CompilerParams(vmem_limit_bytes=42 << 20),
        cost_estimate=cost,
    )(jnp.stack(heads).astype(jnp.int32), *srcs, w, *old)


def cut(pieces):
    def body(*refs):
        k = len(pieces)
        copies = [
            pltpu.make_async_copy(
                refs[i].at[pl.ds(start, n), :], refs[k + i], refs[2 * k].at[i]
            )
            for i, (_, start, n) in enumerate(pieces)
        ]
        for copy in copies:
            copy.start()
        for copy in copies:
            copy.wait()

    return pl.pallas_call(
        body,
        in_specs=[pl.BlockSpec(memory_space=pl.ANY)] * len(pieces),
        out_specs=[pl.BlockSpec(memory_space=pl.ANY)] * len(pieces),
        out_shape=[jax.ShapeDtypeStruct((n, a.shape[1]), a.dtype) for a, _, n in pieces],
        scratch_shapes=[pltpu.SemaphoreType.DMA((len(pieces),))],
        cost_estimate=pl.CostEstimate(flops=0, bytes_accessed=3 << 20, transcendentals=0),
    )(*[a for a, _, _ in pieces])


NT = (((1,), (1,)), ((), ()))


def scan_and_read(got, slice_rows, slots):
    sections, _, dim = got.shape
    head_rows, half = got.shape[1] - slice_rows - slots, slice_rows // 2

    def body(got_ref, out_ref, ends):
        state = jnp.zeros((slice_rows, dim), F32)
        for c in range(sections):
            out_ref[c, :slice_rows, :] = state.astype(BF)
            header = got_ref[c, slice_rows : slice_rows + 16, :].astype(F32)
            factor = header[0:1] + header[1:2] + header[2:3]
            state = factor * state + got_ref[c, :slice_rows, :].astype(F32)
            ends[c * slice_rows : (c + 1) * slice_rows, :] = state.astype(BF)

        @pl.loop(0, sections // 2)
        def _(p):
            asked, named = [], []
            for c in (2 * p, 2 * p + 1):
                asked.append(got_ref[c, slice_rows + head_rows :, :])
                header = got_ref[c, slice_rows : slice_rows + 16, :].astype(F32)
                named.append(header[3:4, :slots])
            asked, named = jnp.concatenate(asked, axis=0), jnp.concatenate(named, axis=1)
            total = jnp.zeros((slice_rows, 2 * slots), F32)
            for j in range(0, sections, 4):
                reads = lax.dot_general(
                    ends[j * slice_rows : (j + 4) * slice_rows, :],
                    asked,
                    NT,
                    preferred_element_type=F32,
                )
                for i in range(4):
                    part = reads[i * slice_rows : (i + 1) * slice_rows]
                    total += jnp.where(named == float(j + i), part, 0.0)
            total = total.astype(BF)
            for k in range(2):
                mine = total[:, k * slots : (k + 1) * slots]
                out_ref[2 * p + k, slice_rows:, :slots] = mine[:half]
                out_ref[2 * p + k, slice_rows:, slots:] = mine[half:]

    return pl.pallas_call(
        body,
        in_specs=[WHOLE],
        out_specs=WHOLE,
        out_shape=jax.ShapeDtypeStruct((sections, slice_rows + half, dim), BF),
        scratch_shapes=[pltpu.VMEM((sections * slice_rows, dim), BF)],
        compiler_params=pltpu.CompilerParams(vmem_limit_bytes=12 << 20),
        cost_estimate=pl.CostEstimate(
            flops=2 * sections * slots * sections * slice_rows * dim,
            bytes_accessed=6 << 20,
            transcendentals=0,
        ),
    )(got)


def retain(queries, within, logs, got, slice_rows, own, kept):
    sections, _, dim = got.shape
    tokens, width = queries.shape
    slots, heads = kept.shape
    per_head = sections // heads

    def body(q_ref, in_ref, l_ref, got_ref, own_ref, k_ref, o_ref, own_held, arrived):
        fetch = pltpu.make_async_copy(own_ref, own_held, arrived)
        fetch.start()
        gains = jnp.exp(l_ref[...])
        gains = jnp.concatenate([gains] * (8 // heads), axis=0).T
        for h in range(heads):
            cols = slice(h * dim, (h + 1) * dim)
            state = got_ref[h * per_head : (h + 1) * per_head, :slice_rows, :].reshape(dim, dim)
            carried = lax.dot_general(q_ref[:, cols], state, NT, preferred_element_type=F32)
            total = in_ref[:, cols] + gains[:, h : h + 1] * carried
            o_ref[:tokens, cols] = total.astype(BF)
        fetch.wait()
        for h in range(heads):
            cols = slice(h * dim, (h + 1) * dim)
            parts = []
            for c in range(h * per_head, (h + 1) * per_head):
                held = got_ref[c, slice_rows:, :].astype(F32)
                parts += [held[:, :slots], held[:, slots:]]
            read = jnp.concatenate(parts, axis=0).T
            mixed = k_ref[:, h : h + 1] * read + own_held[:, cols]
            o_ref[tokens:, cols] = mixed.astype(BF)

    specs = [WHOLE] * 6
    specs[4] = pl.BlockSpec(memory_space=pl.ANY)
    return pl.pallas_call(
        body,
        in_specs=specs,
        out_specs=WHOLE,
        out_shape=jax.ShapeDtypeStruct((tokens + slots, width), BF),
        scratch_shapes=[pltpu.VMEM(own.shape, F32), pltpu.SemaphoreType.DMA],
        compiler_params=pltpu.CompilerParams(vmem_limit_bytes=12 << 20),
        cost_estimate=pl.CostEstimate(
            flops=2 * tokens * width * dim, bytes_accessed=6 << 20, transcendentals=0
        ),
    )(queries, within, logs, got, own, kept)


def gathered_projection(block, split, w):
    me = lax.axis_index("head")
    z, x = me // 2, me % 2
    here, far = lambda d: ((z + d) % 4) * 2 + x, lambda d: ((z + d) % 4) * 2 + 1 - x
    n = block.shape[0]
    third = -(-n // 48) * 16
    whole = lambda s: (s, s, 0, n, 0)

    a1, a2, a3 = up(block), down(block), across(block)
    (total,) = project(n, [block], [whole(0)], [me], w)
    a1, a2, a3, total = lax.optimization_barrier((a1, a2, a3, total))

    b1, b2, b3 = up(a3), down(a2), across(a2)
    width = block.shape[1]
    w_last = lax.dynamic_slice_in_dim(after(w, total), far(2) * width, width, 0)
    (total,) = project(
        total, [a1, a2, a3], [whole(s) for s in range(3)], [here(-1), here(1), far(0)], w
    )
    b1, b2, b3, total, w_last = lax.optimization_barrier((b1, b2, b3, total, w_last))

    c1, c2, c3 = cut([(b1, 0, third), (b3, third, third), (b2, 2 * third, n - 2 * third)])
    c1, c2, c3 = up(c1), down(c2), across(c3)
    (total,) = project(
        total, [b1, b2, b3], [whole(s) for s in range(3)], [far(-1), here(2), far(1)], w
    )
    c1, c2, c3, total = lax.optimization_barrier((c1, c2, c3, total))
    return project(
        total,
        [c1, c2, c3],
        [(0, i, 0, c.shape[0], i * third) for i, c in enumerate((c1, c2, c3))],
        None,
        w_last,
        split,
    )


def shards(
    q_prompt,
    k_prompt,
    v_prompt,
    log_decay,
    prompt_section,
    q_step,
    k_step,
    v_step,
    step_decay,
    w_out,
):
    tokens, heads, dim = q_prompt.shape
    sections = lax.axis_size("ctx")
    rows, steps = q_step.shape[:2]

    at = jnp.arange(tokens)
    upto = (at[:, None] <= at[None, :]).astype(F32)
    cumlog = jnp.dot(log_decay, upto, precision=lax.Precision.HIGHEST)
    last_log = cumlog[:, -1]
    keys = (k_prompt.astype(F32) * jnp.exp(last_log[:, None] - cumlog).T[:, :, None]).astype(BF)
    own_state = jnp.einsum("jxp,jxa->xpa", v_prompt, keys, preferred_element_type=F32)
    total_decay = jnp.exp(last_log)
    slice_rows, slots = heads * dim // sections, rows * steps
    high = lax.reduce_precision(total_decay, 8, 7)
    middle = lax.reduce_precision(total_decay - high, 8, 7)
    parts = jnp.stack([high, middle, total_decay - high - middle], axis=1).astype(BF)
    parts = jnp.broadcast_to(parts[:, None, :, None], (heads, sections // heads, 3, dim))
    named = jnp.broadcast_to(prompt_section, (rows, steps)).reshape(1, 1, slots).astype(BF)
    named = jnp.pad(named, ((0, 0), (0, 0), (0, dim - slots)))
    named = jnp.broadcast_to(named, (sections, 1, dim))
    header = jnp.concatenate([parts.reshape(sections, 3, dim), named], axis=1)
    header = jnp.pad(header, ((0, 0), (0, 12), (0, 0)))
    asked = q_step.reshape(slots, heads, dim).transpose(1, 0, 2)
    asked = jnp.broadcast_to(asked[:, None], (heads, sections // heads, slots, dim))
    sent = jnp.concatenate(
        [
            own_state.astype(BF).reshape(sections, slice_rows, dim),
            header,
            asked.reshape(sections, slots, dim),
        ],
        axis=1,
    )
    got = lax.all_to_all(sent, "ctx", 0, 0)

    q_late, k_late, v_late, cum_late = after((q_prompt, k_prompt, v_prompt, cumlog), sent)
    causal = at[:, None] >= at[None, :]
    decays = jnp.where(
        causal[None], jnp.exp(jnp.minimum(cum_late[:, :, None] - cum_late[:, None, :], 0.0)), 0.0
    )
    scores = jnp.einsum("jsv,csv->sjc", q_late, k_late, preferred_element_type=F32)
    weights = (scores * decays).astype(BF)
    within = jnp.einsum("hnm,mhe->nhe", weights, v_late, preferred_element_type=F32)
    within = within.reshape(tokens, heads * dim)
    queries = q_late.reshape(tokens, heads * dim)
    got, within, queries, cum_late = lax.optimization_barrier((got, within, queries, cum_late))

    sent = scan_and_read(got, slice_rows, slots)
    got = lax.all_to_all(sent, "ctx", 0, 0)

    q_own, k_own, v_own, rates = after((q_step, k_step, v_step, step_decay), sent)
    rates = jnp.transpose(rates, (2, 1, 0))
    logs = [rates[:, 0]]
    for t in range(1, steps):
        logs.append(logs[-1] + rates[:, t])
    step_logs = jnp.stack(logs, axis=1)
    head_logs = jnp.transpose(step_logs, (0, 2, 1))
    turn = jnp.arange(steps)
    seen = turn[:, None] >= turn[None, :]
    gaps = head_logs[:, :, :, None] - head_logs[:, :, None, :]
    step_gains = jnp.where(seen[None, None], jnp.exp(jnp.minimum(gaps, 0.0)), 0.0)
    own = jnp.einsum("rthd,ruhd->rhtu", q_own, k_own, preferred_element_type=F32)
    own = jnp.einsum("rhtu,ruhe->rthe", own * step_gains, v_own.astype(F32))
    own = own.reshape(slots, heads * dim)
    kept = jnp.exp(step_logs).reshape(slots, heads)
    got, own, kept = lax.optimization_barrier((got, own, kept))

    block = retain(queries, within, cum_late, got, slice_rows, own, kept)
    prompt_out, step_out = gathered_projection(block, tokens, w_out)
    return prompt_out, step_out.reshape(rows, steps, w_out.shape[1])


def solution(mesh):
    in_specs = (
        P("ctx", "head", None),
        P("ctx", "head", None),
        P("ctx", "head", None),
        P("head", "ctx"),
        P("ctx", None),
        P("ctx", None, "head", None),
        P("ctx", None, "head", None),
        P("ctx", None, "head", None),
        P("head", None, "ctx"),
        P(None, "head"),
    )
    out_specs = (P("ctx", "head"), P("ctx", None, "head"))
    return jax.shard_map(shards, mesh=mesh, in_specs=in_specs, out_specs=out_specs, check_vma=False)
```

```python
import jax
import jax.numpy as jnp
from jax import lax
from jax.experimental import pallas as pl
from jax.experimental.pallas import tpu as pltpu
from jax.sharding import PartitionSpec as P

BF, F32 = jnp.bfloat16, jnp.float32
WHOLE = pl.BlockSpec(memory_space=pltpu.VMEM)


def up(a):
    return lax.ppermute(a, "head", [(h, (h + 2) % 8) for h in range(8)])


def down(a):
    return lax.ppermute(a, "head", [(h, (h - 2) % 8) for h in range(8)])


def across(a):
    return lax.ppermute(a, "head", [(h, h ^ 1) for h in range(8)])


def after(values, *others):
    return lax.optimization_barrier((values, others))[0]


def project(total, srcs, terms, heads, w, split=None):
    width, columns = srcs[0].shape[1], w.shape[1]
    n_slot = 0 if heads is None else len(heads)
    old = [] if isinstance(total, int) else [total]
    rows = total if isinstance(total, int) else total.shape[0]

    def add(slot, weights, src_refs, old_refs, out_refs):
        for s, i, s0, n, a0 in terms:
            if s != slot:
                continue
            part = jnp.dot(src_refs[i][s0 : s0 + n, :], weights, preferred_element_type=F32)
            if slot:
                part += out_refs[0][a0 : a0 + n, :]
            elif old:
                part += old_refs[0][a0 : a0 + n, :]
            if split is None:
                out_refs[0][a0 : a0 + n, :] = part
                continue
            top = min(max(split - a0, 0), n)
            if top:
                out_refs[0][a0 : a0 + top, :] = part[:top].astype(BF)
            if top < n:
                below = a0 + top - split
                out_refs[1][below : below + n - top, :] = part[top:].astype(BF)

    def body(*refs):
        if heads is None:
            src_refs, w_ref, refs = refs[: len(srcs)], refs[len(srcs)], refs[len(srcs) + 1 :]
            add(0, w_ref[...], src_refs, refs[: len(old)], refs[len(old) :])
            return
        heads_ref, *refs = refs
        src_refs, w_ref, refs = refs[: len(srcs)], refs[len(srcs)], refs[len(srcs) + 1 :]
        w_held, arrived = refs[-2:]
        copies = []
        for slot in range(n_slot):
            first = pl.multiple_of(heads_ref[slot] * width, width)
            copies.append(
                pltpu.make_async_copy(
                    w_ref.at[pl.ds(first, width), :], w_held.at[slot], arrived.at[slot]
                )
            )
            copies[-1].start()
        for slot in range(n_slot):
            copies[slot].wait()
            add(slot, w_held[slot], src_refs, refs[: len(old)], refs[len(old) : -2])

    if split is None:
        out = [jax.ShapeDtypeStruct((rows, columns), F32)]
    else:
        out = [jax.ShapeDtypeStruct((r, columns), BF) for r in (split, rows - split)]
    flops = sum(2 * t[3] * width * columns for t in terms)
    cost = pl.CostEstimate(
        flops=flops, bytes_accessed=max(n_slot, 1) * 2 * width * columns, transcendentals=0
    )
    if heads is None:
        return pl.pallas_call(
            body,
            in_specs=[WHOLE] * (len(srcs) + 1 + len(old)),
            out_specs=[WHOLE] * len(out),
            out_shape=out,
            compiler_params=pltpu.CompilerParams(vmem_limit_bytes=16 << 20),
            cost_estimate=cost,
        )(*srcs, w, *old)
    return pl.pallas_call(
        body,
        in_specs=[pl.BlockSpec(memory_space=pltpu.SMEM)]
        + [WHOLE] * len(srcs)
        + [pl.BlockSpec(memory_space=pltpu.HBM)]
        + [WHOLE] * len(old),
        out_specs=[WHOLE] * len(out),
        out_shape=out,
        scratch_shapes=[
            pltpu.VMEM((n_slot, width, columns), BF),
            pltpu.SemaphoreType.DMA((n_slot,)),
        ],
        compiler_params=pltpu.CompilerParams(vmem_limit_bytes=42 << 20),
        cost_estimate=cost,
    )(jnp.stack(heads).astype(jnp.int32), *srcs, w, *old)


def cut(pieces):
    def body(*refs):
        k = len(pieces)
        copies = [
            pltpu.make_async_copy(
                refs[i].at[pl.ds(start, n), :], refs[k + i], refs[2 * k].at[i]
            )
            for i, (_, start, n) in enumerate(pieces)
        ]
        for copy in copies:
            copy.start()
        for copy in copies:
            copy.wait()

    return pl.pallas_call(
        body,
        in_specs=[pl.BlockSpec(memory_space=pl.ANY)] * len(pieces),
        out_specs=[WHOLE] * len(pieces),
        out_shape=[jax.ShapeDtypeStruct((n, a.shape[1]), a.dtype) for a, _, n in pieces],
        scratch_shapes=[pltpu.SemaphoreType.DMA((len(pieces),))],
        cost_estimate=pl.CostEstimate(flops=0, bytes_accessed=3 << 20, transcendentals=0),
    )(*[a for a, _, _ in pieces])


NT = (((1,), (1,)), ((), ()))


def scan_and_read(got, slice_rows, slots):
    sections, _, dim = got.shape
    head_rows, half = got.shape[1] - slice_rows - slots, slice_rows // 2

    def body(got_ref, out_ref, ends):
        state = jnp.zeros((slice_rows, dim), F32)
        for c in range(sections):
            out_ref[c, :slice_rows, :] = state.astype(BF)
            header = got_ref[c, slice_rows : slice_rows + 16, :].astype(F32)
            factor = header[0:1] + header[1:2] + header[2:3]
            state = factor * state + got_ref[c, :slice_rows, :].astype(F32)
            ends[c * slice_rows : (c + 1) * slice_rows, :] = state.astype(BF)

        @pl.loop(0, sections // 2)
        def _(p):
            asked, named = [], []
            for c in (2 * p, 2 * p + 1):
                asked.append(got_ref[c, slice_rows + head_rows :, :])
                header = got_ref[c, slice_rows : slice_rows + 16, :].astype(F32)
                named.append(header[3:4, :slots])
            asked, named = jnp.concatenate(asked, axis=0), jnp.concatenate(named, axis=1)
            total = jnp.zeros((slice_rows, 2 * slots), F32)
            for j in range(0, sections, 4):
                reads = lax.dot_general(
                    ends[j * slice_rows : (j + 4) * slice_rows, :],
                    asked,
                    NT,
                    preferred_element_type=F32,
                )
                for i in range(4):
                    part = reads[i * slice_rows : (i + 1) * slice_rows]
                    total += jnp.where(named == float(j + i), part, 0.0)
            total = total.astype(BF)
            for k in range(2):
                mine = total[:, k * slots : (k + 1) * slots]
                out_ref[2 * p + k, slice_rows:, :slots] = mine[:half]
                out_ref[2 * p + k, slice_rows:, slots:] = mine[half:]

    return pl.pallas_call(
        body,
        in_specs=[WHOLE],
        out_specs=WHOLE,
        out_shape=jax.ShapeDtypeStruct((sections, slice_rows + half, dim), BF),
        scratch_shapes=[pltpu.VMEM((sections * slice_rows, dim), BF)],
        compiler_params=pltpu.CompilerParams(vmem_limit_bytes=12 << 20),
        cost_estimate=pl.CostEstimate(
            flops=2 * sections * slots * sections * slice_rows * dim,
            bytes_accessed=6 << 20,
            transcendentals=0,
        ),
    )(got)


def retain(queries, within, logs, got, slice_rows, own, kept):
    sections, _, dim = got.shape
    tokens, width = queries.shape
    slots, heads = kept.shape
    per_head = sections // heads

    def body(q_ref, in_ref, l_ref, got_ref, own_ref, k_ref, o_ref, own_held, arrived):
        fetch = pltpu.make_async_copy(own_ref, own_held, arrived)
        fetch.start()
        gains = jnp.exp(l_ref[...])
        gains = jnp.concatenate([gains] * (8 // heads), axis=0).T
        for h in range(heads):
            cols = slice(h * dim, (h + 1) * dim)
            state = got_ref[h * per_head : (h + 1) * per_head, :slice_rows, :].reshape(dim, dim)
            carried = lax.dot_general(q_ref[:, cols], state, NT, preferred_element_type=F32)
            total = in_ref[:, cols] + gains[:, h : h + 1] * carried
            o_ref[:tokens, cols] = total.astype(BF)
        fetch.wait()
        for h in range(heads):
            cols = slice(h * dim, (h + 1) * dim)
            parts = []
            for c in range(h * per_head, (h + 1) * per_head):
                held = got_ref[c, slice_rows:, :].astype(F32)
                parts += [held[:, :slots], held[:, slots:]]
            read = jnp.concatenate(parts, axis=0).T
            mixed = k_ref[:, h : h + 1] * read + own_held[:, cols]
            o_ref[tokens:, cols] = mixed.astype(BF)

    specs = [WHOLE] * 6
    specs[4] = pl.BlockSpec(memory_space=pl.ANY)
    return pl.pallas_call(
        body,
        in_specs=specs,
        out_specs=WHOLE,
        out_shape=jax.ShapeDtypeStruct((tokens + slots, width), BF),
        scratch_shapes=[pltpu.VMEM(own.shape, F32), pltpu.SemaphoreType.DMA],
        compiler_params=pltpu.CompilerParams(vmem_limit_bytes=12 << 20),
        cost_estimate=pl.CostEstimate(
            flops=2 * tokens * width * dim, bytes_accessed=6 << 20, transcendentals=0
        ),
    )(queries, within, logs, got, own, kept)


def gathered_projection(block, split, w):
    me = lax.axis_index("head")
    z, x = me // 2, me % 2
    here, far = lambda d: ((z + d) % 4) * 2 + x, lambda d: ((z + d) % 4) * 2 + 1 - x
    n = block.shape[0]
    third = -(-n // 48) * 16
    whole = lambda s: (s, s, 0, n, 0)

    a1, a2, a3 = up(block), down(block), across(block)
    (total,) = project(n, [block], [whole(0)], [me], w)
    a1, a2, a3, total = lax.optimization_barrier((a1, a2, a3, total))

    b1, b2, b3 = up(a3), down(a2), across(a2)
    width = block.shape[1]
    w_last = lax.dynamic_slice_in_dim(after(w, total), far(2) * width, width, 0)
    (total,) = project(
        total, [a1, a2, a3], [whole(s) for s in range(3)], [here(-1), here(1), far(0)], w
    )
    b1, b2, b3, total, w_last = lax.optimization_barrier((b1, b2, b3, total, w_last))

    c1, c2, c3 = cut([(b1, 0, third), (b3, third, third), (b2, 2 * third, n - 2 * third)])
    c1, c2, c3 = up(c1), down(c2), across(c3)
    (total,) = project(
        total, [b1, b2, b3], [whole(s) for s in range(3)], [far(-1), here(2), far(1)], w
    )
    c1, c2, c3, total = lax.optimization_barrier((c1, c2, c3, total))
    return project(
        total,
        [c1, c2, c3],
        [(0, i, 0, c.shape[0], i * third) for i, c in enumerate((c1, c2, c3))],
        None,
        w_last,
        split,
    )


def shards(
    q_prompt,
    k_prompt,
    v_prompt,
    log_decay,
    prompt_section,
    q_step,
    k_step,
    v_step,
    step_decay,
    w_out,
):
    tokens, heads, dim = q_prompt.shape
    sections = lax.axis_size("ctx")
    rows, steps = q_step.shape[:2]

    at = jnp.arange(tokens)
    upto = (at[:, None] <= at[None, :]).astype(F32)
    cumlog = jnp.dot(log_decay, upto, precision=lax.Precision.HIGHEST)
    last_log = cumlog[:, -1]
    keys = (k_prompt.astype(F32) * jnp.exp(last_log[:, None] - cumlog).T[:, :, None]).astype(BF)
    own_state = jnp.einsum("jxp,jxa->xpa", v_prompt, keys, preferred_element_type=F32)
    total_decay = jnp.exp(last_log)
    slice_rows, slots = heads * dim // sections, rows * steps
    high = lax.reduce_precision(total_decay, 8, 7)
    middle = lax.reduce_precision(total_decay - high, 8, 7)
    parts = jnp.stack([high, middle, total_decay - high - middle], axis=1).astype(BF)
    parts = jnp.broadcast_to(parts[:, None, :, None], (heads, sections // heads, 3, dim))
    named = jnp.broadcast_to(prompt_section, (rows, steps)).reshape(1, 1, slots).astype(BF)
    named = jnp.pad(named, ((0, 0), (0, 0), (0, dim - slots)))
    named = jnp.broadcast_to(named, (sections, 1, dim))
    header = jnp.concatenate([parts.reshape(sections, 3, dim), named], axis=1)
    header = jnp.pad(header, ((0, 0), (0, 12), (0, 0)))
    asked = q_step.reshape(slots, heads, dim).transpose(1, 0, 2)
    asked = jnp.broadcast_to(asked[:, None], (heads, sections // heads, slots, dim))
    sent = jnp.concatenate(
        [
            own_state.astype(BF).reshape(sections, slice_rows, dim),
            header,
            asked.reshape(sections, slots, dim),
        ],
        axis=1,
    )
    got = lax.all_to_all(sent, "ctx", 0, 0)

    q_late, k_late, v_late, cum_late = after((q_prompt, k_prompt, v_prompt, cumlog), sent)
    causal = at[:, None] >= at[None, :]
    decays = jnp.where(
        causal[None], jnp.exp(jnp.minimum(cum_late[:, :, None] - cum_late[:, None, :], 0.0)), 0.0
    )
    scores = jnp.einsum("jsv,csv->sjc", q_late, k_late, preferred_element_type=F32)
    weights = (scores * decays).astype(BF)
    within = jnp.einsum("hnm,mhe->nhe", weights, v_late, preferred_element_type=F32)
    within = within.reshape(tokens, heads * dim)
    queries = q_late.reshape(tokens, heads * dim)
    got, within, queries, cum_late = lax.optimization_barrier((got, within, queries, cum_late))

    sent = scan_and_read(got, slice_rows, slots)
    got = lax.all_to_all(sent, "ctx", 0, 0)

    q_own, k_own, v_own, rates = after((q_step, k_step, v_step, step_decay), sent)
    rates = jnp.transpose(rates, (2, 1, 0))
    logs = [rates[:, 0]]
    for t in range(1, steps):
        logs.append(logs[-1] + rates[:, t])
    step_logs = jnp.stack(logs, axis=1)
    head_logs = jnp.transpose(step_logs, (0, 2, 1))
    turn = jnp.arange(steps)
    seen = turn[:, None] >= turn[None, :]
    gaps = head_logs[:, :, :, None] - head_logs[:, :, None, :]
    step_gains = jnp.where(seen[None, None], jnp.exp(jnp.minimum(gaps, 0.0)), 0.0)
    own = jnp.einsum("rthd,ruhd->rhtu", q_own, k_own, preferred_element_type=F32)
    own = jnp.einsum("rhtu,ruhe->rthe", own * step_gains, v_own.astype(F32))
    own = own.reshape(slots, heads * dim)
    kept = jnp.exp(step_logs).reshape(slots, heads)

    block = retain(queries, within, cum_late, got, slice_rows, own, kept)
    prompt_out, step_out = gathered_projection(block, tokens, w_out)
    return prompt_out, step_out.reshape(rows, steps, w_out.shape[1])


def solution(mesh):
    in_specs = (
        P("ctx", "head", None),
        P("ctx", "head", None),
        P("ctx", "head", None),
        P("head", "ctx"),
        P("ctx", None),
        P("ctx", None, "head", None),
        P("ctx", None, "head", None),
        P("ctx", None, "head", None),
        P("head", None, "ctx"),
        P(None, "head"),
    )
    out_specs = (P("ctx", "head"), P("ctx", None, "head"))
    return jax.shard_map(shards, mesh=mesh, in_specs=in_specs, out_specs=out_specs, check_vma=False)
```

```python
import jax
import jax.numpy as jnp
from jax import lax
from jax.experimental import pallas as pl
from jax.experimental.pallas import tpu as pltpu
from jax.sharding import PartitionSpec as P

BF, F32 = jnp.bfloat16, jnp.float32
WHOLE = pl.BlockSpec(memory_space=pltpu.VMEM)


def up(a):
    return lax.ppermute(a, "head", [(h, (h + 2) % 8) for h in range(8)])


def down(a):
    return lax.ppermute(a, "head", [(h, (h - 2) % 8) for h in range(8)])


def across(a):
    return lax.ppermute(a, "head", [(h, h ^ 1) for h in range(8)])


def after(values, *others):
    return lax.optimization_barrier((values, others))[0]


def project(total, srcs, terms, heads, w, split=None):
    width, columns = srcs[0].shape[1], w.shape[1]
    n_slot = 0 if heads is None else len(heads)
    old = [] if isinstance(total, int) else [total]
    rows = total if isinstance(total, int) else total.shape[0]

    def add(slot, weights, src_refs, old_refs, out_refs):
        for s, i, s0, n, a0 in terms:
            if s != slot:
                continue
            part = jnp.dot(src_refs[i][s0 : s0 + n, :], weights, preferred_element_type=F32)
            if slot:
                part += out_refs[0][a0 : a0 + n, :]
            elif old:
                part += old_refs[0][a0 : a0 + n, :]
            if split is None:
                out_refs[0][a0 : a0 + n, :] = part
                continue
            top = min(max(split - a0, 0), n)
            if top:
                out_refs[0][a0 : a0 + top, :] = part[:top].astype(BF)
            if top < n:
                below = a0 + top - split
                out_refs[1][below : below + n - top, :] = part[top:].astype(BF)

    def body(*refs):
        if heads is None:
            src_refs, w_ref, refs = refs[: len(srcs)], refs[len(srcs)], refs[len(srcs) + 1 :]
            add(0, w_ref[...], src_refs, refs[: len(old)], refs[len(old) :])
            return
        heads_ref, *refs = refs
        src_refs, w_ref, refs = refs[: len(srcs)], refs[len(srcs)], refs[len(srcs) + 1 :]
        w_held, arrived = refs[-2:]
        copies = []
        for slot in range(n_slot):
            first = pl.multiple_of(heads_ref[slot] * width, width)
            copies.append(
                pltpu.make_async_copy(
                    w_ref.at[pl.ds(first, width), :], w_held.at[slot], arrived.at[slot]
                )
            )
            copies[-1].start()
        for slot in range(n_slot):
            copies[slot].wait()
            add(slot, w_held[slot], src_refs, refs[: len(old)], refs[len(old) : -2])

    if split is None:
        out = [jax.ShapeDtypeStruct((rows, columns), F32)]
    else:
        out = [jax.ShapeDtypeStruct((r, columns), BF) for r in (split, rows - split)]
    flops = sum(2 * t[3] * width * columns for t in terms)
    cost = pl.CostEstimate(
        flops=flops >> 10, bytes_accessed=1 << 10, transcendentals=0
    )
    if heads is None:
        return pl.pallas_call(
            body,
            in_specs=[WHOLE] * (len(srcs) + 1 + len(old)),
            out_specs=[WHOLE] * len(out),
            out_shape=out,
            compiler_params=pltpu.CompilerParams(vmem_limit_bytes=16 << 20),
            cost_estimate=cost,
        )(*srcs, w, *old)
    return pl.pallas_call(
        body,
        in_specs=[pl.BlockSpec(memory_space=pltpu.SMEM)]
        + [WHOLE] * len(srcs)
        + [pl.BlockSpec(memory_space=pltpu.HBM)]
        + [WHOLE] * len(old),
        out_specs=[WHOLE] * len(out),
        out_shape=out,
        scratch_shapes=[
            pltpu.VMEM((n_slot, width, columns), BF),
            pltpu.SemaphoreType.DMA((n_slot,)),
        ],
        compiler_params=pltpu.CompilerParams(vmem_limit_bytes=42 << 20),
        cost_estimate=cost,
    )(jnp.stack(heads).astype(jnp.int32), *srcs, w, *old)


NT = (((1,), (1,)), ((), ()))


def scan_and_read(got, slice_rows, slots):
    sections, _, dim = got.shape
    head_rows, half = got.shape[1] - slice_rows - slots, slice_rows // 2

    def body(got_ref, out_ref, ends):
        state = jnp.zeros((slice_rows, dim), F32)
        for c in range(sections):
            out_ref[c, :slice_rows, :] = state.astype(BF)
            header = got_ref[c, slice_rows : slice_rows + 16, :].astype(F32)
            factor = header[0:1] + header[1:2] + header[2:3]
            state = factor * state + got_ref[c, :slice_rows, :].astype(F32)
            ends[c * slice_rows : (c + 1) * slice_rows, :] = state.astype(BF)

        @pl.loop(0, sections // 2)
        def _(p):
            asked, named = [], []
            for c in (2 * p, 2 * p + 1):
                asked.append(got_ref[c, slice_rows + head_rows :, :])
                header = got_ref[c, slice_rows : slice_rows + 16, :].astype(F32)
                named.append(header[3:4, :slots])
            asked, named = jnp.concatenate(asked, axis=0), jnp.concatenate(named, axis=1)
            total = jnp.zeros((slice_rows, 2 * slots), F32)
            for j in range(0, sections, 4):
                reads = lax.dot_general(
                    ends[j * slice_rows : (j + 4) * slice_rows, :],
                    asked,
                    NT,
                    preferred_element_type=F32,
                )
                for i in range(4):
                    part = reads[i * slice_rows : (i + 1) * slice_rows]
                    total += jnp.where(named == float(j + i), part, 0.0)
            total = total.astype(BF)
            for k in range(2):
                mine = total[:, k * slots : (k + 1) * slots]
                out_ref[2 * p + k, slice_rows:, :slots] = mine[:half]
                out_ref[2 * p + k, slice_rows:, slots:] = mine[half:]

    return pl.pallas_call(
        body,
        in_specs=[WHOLE],
        out_specs=WHOLE,
        out_shape=jax.ShapeDtypeStruct((sections, slice_rows + half, dim), BF),
        scratch_shapes=[pltpu.VMEM((sections * slice_rows, dim), BF)],
        compiler_params=pltpu.CompilerParams(vmem_limit_bytes=12 << 20),
        cost_estimate=pl.CostEstimate(
            flops=2 * sections * slots * sections * slice_rows * dim,
            bytes_accessed=6 << 20,
            transcendentals=0,
        ),
    )(got)


def retain(queries, within, logs, got, slice_rows, own, kept):
    sections, _, dim = got.shape
    tokens, width = queries.shape
    slots, heads = kept.shape
    per_head = sections // heads

    n = tokens + slots
    upper = n // 2

    def body(q_ref, in_ref, l_ref, got_ref, own_ref, k_ref, o_ref, t_ref, b_ref, own_held, arrived):
        fetch = pltpu.make_async_copy(own_ref, own_held, arrived)
        fetch.start()
        gains = jnp.exp(l_ref[...])
        gains = jnp.concatenate([gains] * (8 // heads), axis=0).T
        for h in range(heads):
            cols = slice(h * dim, (h + 1) * dim)
            state = got_ref[h * per_head : (h + 1) * per_head, :slice_rows, :].reshape(dim, dim)
            carried = lax.dot_general(q_ref[:, cols], state, NT, preferred_element_type=F32)
            total = in_ref[:, cols] + gains[:, h : h + 1] * carried
            o_ref[:tokens, cols] = total.astype(BF)
        fetch.wait()
        for h in range(heads):
            cols = slice(h * dim, (h + 1) * dim)
            parts = []
            for c in range(h * per_head, (h + 1) * per_head):
                held = got_ref[c, slice_rows:, :].astype(F32)
                parts += [held[:, :slots], held[:, slots:]]
            read = jnp.concatenate(parts, axis=0).T
            mixed = k_ref[:, h : h + 1] * read + own_held[:, cols]
            o_ref[tokens:, cols] = mixed.astype(BF)
        t_ref[...] = o_ref[:upper, :]
        b_ref[...] = o_ref[upper:, :]

    specs = [WHOLE] * 6
    specs[4] = pl.BlockSpec(memory_space=pl.ANY)
    return pl.pallas_call(
        body,
        in_specs=specs,
        out_specs=[WHOLE] * 3,
        out_shape=[jax.ShapeDtypeStruct((r, width), BF) for r in (n, upper, n - upper)],
        scratch_shapes=[pltpu.VMEM(own.shape, F32), pltpu.SemaphoreType.DMA],
        compiler_params=pltpu.CompilerParams(vmem_limit_bytes=12 << 20),
        cost_estimate=pl.CostEstimate(
            flops=2 * tokens * width * dim, bytes_accessed=6 << 20, transcendentals=0
        ),
    )(queries, within, logs, got, own, kept)


def gathered_projection(blocks, split, w):
    me = lax.axis_index("head")
    z, x = me // 2, me % 2
    here, far = lambda d: ((z + d) % 4) * 2 + x, lambda d: ((z + d) % 4) * 2 + 1 - x
    block, top, bottom = blocks
    n, h = block.shape[0], top.shape[0]
    width = block.shape[1]
    whole = lambda slot, i: [(slot, i, 0, n, 0)]
    halves = lambda slot, i: [(slot, i, 0, h, 0), (slot, i + 1, 0, n - h, h)]

    down_top, down_bottom = down(top), down(bottom)
    from_below, from_side = up(block), across(block)
    (total,) = project(n, [block], whole(0, 0), [me], w)

    down_top, total = lax.optimization_barrier((down_top, total))
    side_below = up(after(from_side, down_bottom))
    side_top, far_bottom = across(down_top), down(down_bottom)
    side_bottom, far_top = across(after(down_bottom, from_below)), down(after(down_top, from_below))
    (total,) = project(
        total,
        [from_below, down_top, down_bottom, from_side],
        whole(0, 0) + halves(1, 1) + whole(2, 3),
        [here(-1), here(1), far(0)],
        w,
    )

    side_top, total = lax.optimization_barrier((side_top, total))
    last_top = down(side_top)
    last_bottom = across(far_bottom)
    w_last = lax.dynamic_slice_in_dim(after(w, total), far(2) * width, width, 0)
    (total,) = project(
        total,
        [side_below, far_top, far_bottom, side_top, side_bottom],
        whole(0, 0) + halves(1, 1) + halves(2, 3),
        [far(-1), here(2), far(1)],
        w,
    )
    last_top, last_bottom, total, w_last = lax.optimization_barrier(
        (last_top, last_bottom, total, w_last)
    )
    return project(total, [last_top, last_bottom], halves(0, 0), None, w_last, split)


def shards(
    q_prompt,
    k_prompt,
    v_prompt,
    log_decay,
    prompt_section,
    q_step,
    k_step,
    v_step,
    step_decay,
    w_out,
):
    tokens, heads, dim = q_prompt.shape
    sections = lax.axis_size("ctx")
    rows, steps = q_step.shape[:2]

    at = jnp.arange(tokens)
    upto = (at[:, None] <= at[None, :]).astype(F32)
    cumlog = jnp.dot(log_decay, upto, precision=lax.Precision.HIGHEST)
    last_log = cumlog[:, -1]
    keys = (k_prompt.astype(F32) * jnp.exp(last_log[:, None] - cumlog).T[:, :, None]).astype(BF)
    own_state = jnp.einsum("jxp,jxa->xpa", v_prompt, keys, preferred_element_type=F32)
    total_decay = jnp.exp(last_log)
    slice_rows, slots = heads * dim // sections, rows * steps
    high = lax.reduce_precision(total_decay, 8, 7)
    middle = lax.reduce_precision(total_decay - high, 8, 7)
    parts = jnp.stack([high, middle, total_decay - high - middle], axis=1).astype(BF)
    parts = jnp.broadcast_to(parts[:, None, :, None], (heads, sections // heads, 3, dim))
    named = jnp.broadcast_to(prompt_section, (rows, steps)).reshape(1, 1, slots).astype(BF)
    named = jnp.pad(named, ((0, 0), (0, 0), (0, dim - slots)))
    named = jnp.broadcast_to(named, (sections, 1, dim))
    header = jnp.concatenate([parts.reshape(sections, 3, dim), named], axis=1)
    header = jnp.pad(header, ((0, 0), (0, 12), (0, 0)))
    asked = q_step.reshape(slots, heads, dim).transpose(1, 0, 2)
    asked = jnp.broadcast_to(asked[:, None], (heads, sections // heads, slots, dim))
    sent = jnp.concatenate(
        [
            own_state.astype(BF).reshape(sections, slice_rows, dim),
            header,
            asked.reshape(sections, slots, dim),
        ],
        axis=1,
    )
    got = lax.all_to_all(sent, "ctx", 0, 0)

    q_late, k_late, v_late, cum_late = after((q_prompt, k_prompt, v_prompt, cumlog), sent)
    causal = at[:, None] >= at[None, :]
    decays = jnp.where(
        causal[None], jnp.exp(jnp.minimum(cum_late[:, :, None] - cum_late[:, None, :], 0.0)), 0.0
    )
    scores = jnp.einsum("jsv,csv->sjc", q_late, k_late, preferred_element_type=F32)
    weights = (scores * decays).astype(BF)
    within = jnp.einsum("hnm,mhe->nhe", weights, v_late, preferred_element_type=F32)
    within = within.reshape(tokens, heads * dim)
    queries = q_late.reshape(tokens, heads * dim)
    got, within, queries, cum_late = lax.optimization_barrier((got, within, queries, cum_late))

    sent = scan_and_read(got, slice_rows, slots)
    got = lax.all_to_all(sent, "ctx", 0, 0)

    q_own, k_own, v_own, rates = after((q_step, k_step, v_step, step_decay), sent)
    rates = jnp.transpose(rates, (2, 1, 0))
    logs = [rates[:, 0]]
    for t in range(1, steps):
        logs.append(logs[-1] + rates[:, t])
    step_logs = jnp.stack(logs, axis=1)
    head_logs = jnp.transpose(step_logs, (0, 2, 1))
    turn = jnp.arange(steps)
    seen = turn[:, None] >= turn[None, :]
    gaps = head_logs[:, :, :, None] - head_logs[:, :, None, :]
    step_gains = jnp.where(seen[None, None], jnp.exp(jnp.minimum(gaps, 0.0)), 0.0)
    own = jnp.einsum("rthd,ruhd->rhtu", q_own, k_own, preferred_element_type=F32)
    own = jnp.einsum("rhtu,ruhe->rthe", own * step_gains, v_own.astype(F32))
    own = own.reshape(slots, heads * dim)
    kept = jnp.exp(step_logs).reshape(slots, heads)

    blocks = retain(queries, within, cum_late, got, slice_rows, own, kept)
    prompt_out, step_out = gathered_projection(blocks, tokens, w_out)
    return prompt_out, step_out.reshape(rows, steps, w_out.shape[1])


def solution(mesh):
    in_specs = (
        P("ctx", "head", None),
        P("ctx", "head", None),
        P("ctx", "head", None),
        P("head", "ctx"),
        P("ctx", None),
        P("ctx", None, "head", None),
        P("ctx", None, "head", None),
        P("ctx", None, "head", None),
        P("head", None, "ctx"),
        P(None, "head"),
    )
    out_specs = (P("ctx", "head"), P("ctx", None, "head"))
    return jax.shard_map(shards, mesh=mesh, in_specs=in_specs, out_specs=out_specs, check_vma=False)
```

```python
import jax
import jax.numpy as jnp
from jax import lax
from jax.experimental import pallas as pl
from jax.experimental.pallas import tpu as pltpu
from jax.sharding import PartitionSpec as P

BF, F32 = jnp.bfloat16, jnp.float32
WHOLE = pl.BlockSpec(memory_space=pltpu.VMEM)


def up(a):
    return lax.ppermute(a, "head", [(h, (h + 2) % 8) for h in range(8)])


def down(a):
    return lax.ppermute(a, "head", [(h, (h - 2) % 8) for h in range(8)])


def across(a):
    return lax.ppermute(a, "head", [(h, h ^ 1) for h in range(8)])


def after(values, *others):
    return lax.optimization_barrier((values, others))[0]


def project(total, srcs, terms, heads, w, split=None, steps=None):
    width, columns = srcs[0].shape[1], w.shape[1]
    n_slot = 0 if heads is None else len(heads)
    old = [] if isinstance(total, int) else [total]
    rows = total if isinstance(total, int) else total.shape[0]

    def add(slot, weights, src_refs, old_refs, out_refs):
        for s, i, s0, n, a0 in terms:
            if s != slot:
                continue
            part = jnp.dot(src_refs[i][s0 : s0 + n, :], weights, preferred_element_type=F32)
            if slot:
                part += out_refs[0][a0 : a0 + n, :]
            elif old:
                part += old_refs[0][a0 : a0 + n, :]
            if split is None:
                out_refs[0][a0 : a0 + n, :] = part
                continue
            top = min(max(split - a0, 0), n)
            if top:
                out_refs[0][a0 : a0 + top, :] = part[:top].astype(BF)
            if top < n:
                below = a0 + top - split
                first, some = below // steps, (n - top) // steps
                rest = part[top:].reshape(some, steps, columns)
                out_refs[1][first : first + some] = rest.astype(BF)

    def body(*refs):
        if heads is None:
            src_refs, w_ref, refs = refs[: len(srcs)], refs[len(srcs)], refs[len(srcs) + 1 :]
            add(0, w_ref[...], src_refs, refs[: len(old)], refs[len(old) :])
            return
        heads_ref, *refs = refs
        src_refs, w_ref, refs = refs[: len(srcs)], refs[len(srcs)], refs[len(srcs) + 1 :]
        w_held, arrived = refs[-2:]
        copies = []
        for slot in range(n_slot):
            first = pl.multiple_of(heads_ref[slot] * width, width)
            copies.append(
                pltpu.make_async_copy(
                    w_ref.at[pl.ds(first, width), :], w_held.at[slot], arrived.at[slot]
                )
            )
            copies[-1].start()
        for slot in range(n_slot):
            copies[slot].wait()
            add(slot, w_held[slot], src_refs, refs[: len(old)], refs[len(old) : -2])

    if split is None:
        out = [jax.ShapeDtypeStruct((rows, columns), F32)]
    else:
        shapes = (split, columns), ((rows - split) // steps, steps, columns)
        out = [jax.ShapeDtypeStruct(shape, BF) for shape in shapes]
    flops = sum(2 * t[3] * width * columns for t in terms)
    cost = pl.CostEstimate(
        flops=flops >> 10, bytes_accessed=1 << 10, transcendentals=0
    )
    if heads is None:
        return pl.pallas_call(
            body,
            in_specs=[WHOLE] * (len(srcs) + 1 + len(old)),
            out_specs=[WHOLE] * len(out),
            out_shape=out,
            compiler_params=pltpu.CompilerParams(vmem_limit_bytes=16 << 20),
            cost_estimate=cost,
        )(*srcs, w, *old)
    return pl.pallas_call(
        body,
        in_specs=[pl.BlockSpec(memory_space=pltpu.SMEM)]
        + [WHOLE] * len(srcs)
        + [pl.BlockSpec(memory_space=pltpu.HBM)]
        + [WHOLE] * len(old),
        out_specs=[WHOLE] * len(out),
        out_shape=out,
        scratch_shapes=[
            pltpu.VMEM((n_slot, width, columns), BF),
            pltpu.SemaphoreType.DMA((n_slot,)),
        ],
        compiler_params=pltpu.CompilerParams(vmem_limit_bytes=42 << 20),
        cost_estimate=cost,
    )(jnp.stack(heads).astype(jnp.int32), *srcs, w, *old)


NT = (((1,), (1,)), ((), ()))


def first_parcels(own_state, parts, named, queries):
    heads, dim, _ = own_state.shape
    slots, rows = queries.shape[1], named.shape[1]
    count = lax.axis_size("ctx")
    per_head = count // heads
    slice_rows = heads * dim // count

    def body(s_ref, p_ref, n_ref, q_ref, o_ref):
        row = lax.broadcasted_iota(jnp.int32, (rows, slots), 0)
        lane = lax.broadcasted_iota(jnp.int32, (rows, slots), 1)
        first = row * (slots // rows)
        mine = (lane >= first) & (lane < first + slots // rows)
        sections = jnp.broadcast_to(n_ref[...].astype(F32), (8, rows)).astype(BF)
        sections = jnp.dot(sections, mine.astype(BF), preferred_element_type=F32)[:1]
        sections = jnp.concatenate([sections, jnp.zeros((1, dim - slots), F32)], axis=1)
        line = lax.broadcasted_iota(jnp.int32, (16, dim), 0)
        for h in range(heads):
            header = jnp.where(line == 3, sections, 0.0)
            for i in range(3):
                header = jnp.where(line == i, p_ref[h : h + 1, i : i + 1], header)
            header = header.astype(BF)
            for k in range(per_head):
                c = h * per_head + k
                o_ref[c, :slice_rows, :] = s_ref[h, k * slice_rows : (k + 1) * slice_rows, :]
                o_ref[c, slice_rows : slice_rows + 16, :] = header
                o_ref[c, slice_rows + 16 :, :] = q_ref[h]

    return pl.pallas_call(
        body,
        in_specs=[WHOLE] * 4,
        out_specs=WHOLE,
        out_shape=jax.ShapeDtypeStruct((count, slice_rows + 16 + slots, dim), BF),
        compiler_params=pltpu.CompilerParams(vmem_limit_bytes=12 << 20),
        cost_estimate=pl.CostEstimate(flops=0, bytes_accessed=3 << 20, transcendentals=0),
    )(own_state, parts, named, queries)


def scan_and_read(got, slice_rows, slots):
    sections, _, dim = got.shape
    head_rows, half = got.shape[1] - slice_rows - slots, slice_rows // 2

    def body(got_ref, out_ref, ends):
        state = jnp.zeros((slice_rows, dim), F32)
        for c in range(sections):
            out_ref[c, :slice_rows, :] = state.astype(BF)
            header = got_ref[c, slice_rows : slice_rows + 16, :].astype(F32)
            factor = header[0:1] + header[1:2] + header[2:3]
            state = factor * state + got_ref[c, :slice_rows, :].astype(F32)
            ends[c * slice_rows : (c + 1) * slice_rows, :] = state.astype(BF)

        @pl.loop(0, sections // 2)
        def _(p):
            asked, named = [], []
            for c in (2 * p, 2 * p + 1):
                asked.append(got_ref[c, slice_rows + head_rows :, :])
                header = got_ref[c, slice_rows : slice_rows + 16, :].astype(F32)
                named.append(header[3:4, :slots])
            asked, named = jnp.concatenate(asked, axis=0), jnp.concatenate(named, axis=1)
            total = jnp.zeros((slice_rows, 2 * slots), F32)
            for j in range(0, sections, 4):
                reads = lax.dot_general(
                    ends[j * slice_rows : (j + 4) * slice_rows, :],
                    asked,
                    NT,
                    preferred_element_type=F32,
                )
                for i in range(4):
                    part = reads[i * slice_rows : (i + 1) * slice_rows]
                    total += jnp.where(named == float(j + i), part, 0.0)
            total = total.astype(BF)
            for k in range(2):
                mine = total[:, k * slots : (k + 1) * slots]
                out_ref[2 * p + k, slice_rows:, :slots] = mine[:half]
                out_ref[2 * p + k, slice_rows:, slots:] = mine[half:]

    return pl.pallas_call(
        body,
        in_specs=[WHOLE],
        out_specs=WHOLE,
        out_shape=jax.ShapeDtypeStruct((sections, slice_rows + half, dim), BF),
        scratch_shapes=[pltpu.VMEM((sections * slice_rows, dim), BF)],
        compiler_params=pltpu.CompilerParams(vmem_limit_bytes=58 << 20),
        cost_estimate=pl.CostEstimate(
            flops=2 * sections * slots * sections * slice_rows * dim,
            bytes_accessed=6 << 20,
            transcendentals=0,
        ),
    )(got)


def retain(queries, within, logs, got, slice_rows, own, kept):
    sections, _, dim = got.shape
    tokens, width = queries.shape
    slots, heads = kept.shape
    per_head = sections // heads

    n = tokens + slots
    upper = n // 2

    def body(q_ref, in_ref, l_ref, got_ref, own_ref, k_ref, o_ref, t_ref, b_ref, own_held, arrived):
        fetch = pltpu.make_async_copy(own_ref, own_held, arrived)
        fetch.start()
        gains = jnp.exp(l_ref[...])
        gains = jnp.concatenate([gains] * (8 // heads), axis=0).T
        for h in range(heads):
            cols = slice(h * dim, (h + 1) * dim)
            state = got_ref[h * per_head : (h + 1) * per_head, :slice_rows, :].reshape(dim, dim)
            carried = lax.dot_general(q_ref[:, cols], state, NT, preferred_element_type=F32)
            total = in_ref[:, cols] + gains[:, h : h + 1] * carried
            o_ref[:tokens, cols] = total.astype(BF)
        fetch.wait()
        for h in range(heads):
            cols = slice(h * dim, (h + 1) * dim)
            parts = []
            for c in range(h * per_head, (h + 1) * per_head):
                held = got_ref[c, slice_rows:, :].astype(F32)
                parts += [held[:, :slots], held[:, slots:]]
            read = jnp.concatenate(parts, axis=0).T
            mixed = k_ref[:, h : h + 1] * read + own_held[:, cols]
            o_ref[tokens:, cols] = mixed.astype(BF)
        t_ref[...] = o_ref[:upper, :]
        b_ref[...] = o_ref[upper:, :]

    specs = [WHOLE] * 6
    specs[4] = pl.BlockSpec(memory_space=pl.ANY)
    return pl.pallas_call(
        body,
        in_specs=specs,
        out_specs=[WHOLE] * 3,
        out_shape=[jax.ShapeDtypeStruct((r, width), BF) for r in (n, upper, n - upper)],
        scratch_shapes=[pltpu.VMEM(own.shape, F32), pltpu.SemaphoreType.DMA],
        compiler_params=pltpu.CompilerParams(vmem_limit_bytes=12 << 20),
        cost_estimate=pl.CostEstimate(
            flops=2 * tokens * width * dim, bytes_accessed=6 << 20, transcendentals=0
        ),
    )(queries, within, logs, got, own, kept)


def gathered_projection(blocks, split, steps, w):
    me = lax.axis_index("head")
    z, x = me // 2, me % 2
    here, far = lambda d: ((z + d) % 4) * 2 + x, lambda d: ((z + d) % 4) * 2 + 1 - x
    block, top, bottom = blocks
    n, h = block.shape[0], top.shape[0]
    width = block.shape[1]
    whole = lambda slot, i: [(slot, i, 0, n, 0)]
    halves = lambda slot, i: [(slot, i, 0, h, 0), (slot, i + 1, 0, n - h, h)]

    down_top, down_bottom = down(top), down(bottom)
    from_below, from_side = up(block), across(block)
    (total,) = project(n, [block], whole(0, 0), [me], w)

    down_top, total = lax.optimization_barrier((down_top, total))
    side_below = up(after(from_side, down_bottom))
    side_top, far_bottom = across(down_top), down(down_bottom)
    side_bottom, far_top = across(after(down_bottom, from_below)), down(after(down_top, from_below))
    (total,) = project(
        total,
        [from_below, down_top, down_bottom, from_side],
        whole(0, 0) + halves(1, 1) + whole(2, 3),
        [here(-1), here(1), far(0)],
        w,
    )

    side_top, total = lax.optimization_barrier((side_top, total))
    last_top = down(side_top)
    last_bottom = across(far_bottom)
    w_last = lax.dynamic_slice_in_dim(after(w, total), far(2) * width, width, 0)
    (total,) = project(
        total,
        [side_below, far_top, far_bottom, side_top, side_bottom],
        whole(0, 0) + halves(1, 1) + halves(2, 3),
        [far(-1), here(2), far(1)],
        w,
    )
    last_top, last_bottom, total, w_last = lax.optimization_barrier(
        (last_top, last_bottom, total, w_last)
    )
    return project(total, [last_top, last_bottom], halves(0, 0), None, w_last, split, steps)


def shards(
    q_prompt,
    k_prompt,
    v_prompt,
    log_decay,
    prompt_section,
    q_step,
    k_step,
    v_step,
    step_decay,
    w_out,
):
    tokens, heads, dim = q_prompt.shape
    sections = lax.axis_size("ctx")
    rows, steps = q_step.shape[:2]

    at = jnp.arange(tokens)
    upto = (at[:, None] <= at[None, :]).astype(F32)
    cumlog = jnp.dot(log_decay, upto, precision=lax.Precision.HIGHEST)
    last_log = cumlog[:, -1]
    keys = (k_prompt.astype(F32) * jnp.exp(last_log[:, None] - cumlog).T[:, :, None]).astype(BF)
    own_state = jnp.einsum("jxp,jxa->xpa", v_prompt, keys, preferred_element_type=F32)
    total_decay = jnp.exp(last_log)
    slice_rows, slots = heads * dim // sections, rows * steps
    high = lax.reduce_precision(total_decay, 8, 7)
    middle = lax.reduce_precision(total_decay - high, 8, 7)
    parts = jnp.stack([high, middle, total_decay - high - middle], axis=1)
    asked = q_step.reshape(slots, heads, dim).transpose(1, 0, 2)
    sent = first_parcels(own_state.astype(BF), parts, prompt_section.reshape(1, rows), asked)
    got = lax.all_to_all(sent, "ctx", 0, 0)

    q_late, k_late, v_late, cum_late = after((q_prompt, k_prompt, v_prompt, cumlog), sent)
    causal = at[:, None] >= at[None, :]
    decays = jnp.where(
        causal[None], jnp.exp(jnp.minimum(cum_late[:, :, None] - cum_late[:, None, :], 0.0)), 0.0
    )
    scores = jnp.einsum("jsv,csv->sjc", q_late, k_late, preferred_element_type=F32)
    weights = (scores * decays).astype(BF)
    within = jnp.einsum("hnm,mhe->nhe", weights, v_late, preferred_element_type=F32)
    within = within.reshape(tokens, heads * dim)
    queries = q_late.reshape(tokens, heads * dim)
    got, within, queries, cum_late = lax.optimization_barrier((got, within, queries, cum_late))

    sent = scan_and_read(got, slice_rows, slots)
    got = lax.all_to_all(sent, "ctx", 0, 0)

    q_own, k_own, v_own, rates = after((q_step, k_step, v_step, step_decay), sent)
    rates = jnp.transpose(rates, (2, 1, 0))
    logs = [rates[:, 0]]
    for t in range(1, steps):
        logs.append(logs[-1] + rates[:, t])
    step_logs = jnp.stack(logs, axis=1)
    head_logs = jnp.transpose(step_logs, (0, 2, 1))
    turn = jnp.arange(steps)
    seen = turn[:, None] >= turn[None, :]
    gaps = head_logs[:, :, :, None] - head_logs[:, :, None, :]
    step_gains = jnp.where(seen[None, None], jnp.exp(jnp.minimum(gaps, 0.0)), 0.0)
    own = jnp.einsum("rthd,ruhd->rhtu", q_own, k_own, preferred_element_type=F32)
    own = jnp.einsum("rhtu,ruhe->rthe", own * step_gains, v_own.astype(F32))
    own = own.reshape(slots, heads * dim)
    kept = jnp.exp(step_logs).reshape(slots, heads)

    blocks = retain(queries, within, cum_late, got, slice_rows, own, kept)
    return tuple(gathered_projection(blocks, tokens, steps, w_out))


def solution(mesh):
    in_specs = (
        P("ctx", "head", None),
        P("ctx", "head", None),
        P("ctx", "head", None),
        P("head", "ctx"),
        P("ctx", None),
        P("ctx", None, "head", None),
        P("ctx", None, "head", None),
        P("ctx", None, "head", None),
        P("head", None, "ctx"),
        P(None, "head"),
    )
    out_specs = (P("ctx", "head"), P("ctx", None, "head"))
    return jax.shard_map(shards, mesh=mesh, in_specs=in_specs, out_specs=out_specs, check_vma=False)
```

```python
import jax
import jax.numpy as jnp
from jax import lax
from jax.experimental import pallas as pl
from jax.experimental.pallas import tpu as pltpu
from jax.sharding import PartitionSpec as P

BF, F32 = jnp.bfloat16, jnp.float32
WHOLE = pl.BlockSpec(memory_space=pltpu.VMEM)


def up(a):
    return lax.ppermute(a, "head", [(h, (h + 2) % 8) for h in range(8)])


def down(a):
    return lax.ppermute(a, "head", [(h, (h - 2) % 8) for h in range(8)])


def across(a):
    return lax.ppermute(a, "head", [(h, h ^ 1) for h in range(8)])


def after(values, *others):
    return lax.optimization_barrier((values, others))[0]


def project(total, srcs, terms, heads, w, split=None, steps=None):
    width, columns = srcs[0].shape[1], w.shape[1]
    n_slot = 0 if heads is None else len(heads)
    old = [] if isinstance(total, int) else [total]
    rows = total if isinstance(total, int) else total.shape[0]

    def add(slot, weights, src_refs, old_refs, out_refs):
        for s, i, s0, n, a0 in terms:
            if s != slot:
                continue
            part = jnp.dot(src_refs[i][s0 : s0 + n, :], weights, preferred_element_type=F32)
            if slot:
                part += out_refs[0][a0 : a0 + n, :]
            elif old:
                part += old_refs[0][a0 : a0 + n, :]
            if split is None:
                out_refs[0][a0 : a0 + n, :] = part
                continue
            top = min(max(split - a0, 0), n)
            if top:
                out_refs[0][a0 : a0 + top, :] = part[:top].astype(BF)
            if top < n:
                below = a0 + top - split
                first, some = below // steps, (n - top) // steps
                rest = part[top:].reshape(some, steps, columns)
                out_refs[1][first : first + some] = rest.astype(BF)

    def body(*refs):
        if heads is None:
            src_refs, w_ref, refs = refs[: len(srcs)], refs[len(srcs)], refs[len(srcs) + 1 :]
            add(0, w_ref[...], src_refs, refs[: len(old)], refs[len(old) :])
            return
        heads_ref, *refs = refs
        src_refs, w_ref, refs = refs[: len(srcs)], refs[len(srcs)], refs[len(srcs) + 1 :]
        w_held, arrived = refs[-2:]
        copies = []
        for slot in range(n_slot):
            first = pl.multiple_of(heads_ref[slot] * width, width)
            copies.append(
                pltpu.make_async_copy(
                    w_ref.at[pl.ds(first, width), :], w_held.at[slot], arrived.at[slot]
                )
            )
            copies[-1].start()
        for slot in range(n_slot):
            copies[slot].wait()
            add(slot, w_held[slot], src_refs, refs[: len(old)], refs[len(old) : -2])

    if split is None:
        out = [jax.ShapeDtypeStruct((rows, columns), F32)]
    else:
        shapes = (split, columns), ((rows - split) // steps, steps, columns)
        out = [jax.ShapeDtypeStruct(shape, BF) for shape in shapes]
    flops = sum(2 * t[3] * width * columns for t in terms)
    cost = pl.CostEstimate(
        flops=flops >> 10, bytes_accessed=1 << 10, transcendentals=0
    )
    if heads is None:
        return pl.pallas_call(
            body,
            in_specs=[WHOLE] * (len(srcs) + 1 + len(old)),
            out_specs=[WHOLE] * len(out),
            out_shape=out,
            compiler_params=pltpu.CompilerParams(vmem_limit_bytes=16 << 20),
            cost_estimate=cost,
        )(*srcs, w, *old)
    return pl.pallas_call(
        body,
        in_specs=[pl.BlockSpec(memory_space=pltpu.SMEM)]
        + [WHOLE] * len(srcs)
        + [pl.BlockSpec(memory_space=pltpu.HBM)]
        + [WHOLE] * len(old),
        out_specs=[WHOLE] * len(out),
        out_shape=out,
        scratch_shapes=[
            pltpu.VMEM((n_slot, width, columns), BF),
            pltpu.SemaphoreType.DMA((n_slot,)),
        ],
        compiler_params=pltpu.CompilerParams(vmem_limit_bytes=42 << 20),
        cost_estimate=cost,
    )(jnp.stack(heads).astype(jnp.int32), *srcs, w, *old)


NT = (((1,), (1,)), ((), ()))


def first_parcels(own_state, parts, named, queries):
    heads, dim, _ = own_state.shape
    slots, rows = queries.shape[1], named.shape[1]
    count = lax.axis_size("ctx")
    per_head = count // heads
    slice_rows = heads * dim // count

    def body(s_ref, p_ref, n_ref, q_ref, o_ref):
        row = lax.broadcasted_iota(jnp.int32, (rows, slots), 0)
        lane = lax.broadcasted_iota(jnp.int32, (rows, slots), 1)
        first = row * (slots // rows)
        mine = (lane >= first) & (lane < first + slots // rows)
        sections = jnp.broadcast_to(n_ref[...].astype(F32), (8, rows)).astype(BF)
        sections = jnp.dot(sections, mine.astype(BF), preferred_element_type=F32)[:1]
        sections = jnp.concatenate([sections, jnp.zeros((1, dim - slots), F32)], axis=1)
        line = lax.broadcasted_iota(jnp.int32, (8, dim), 0)
        for h in range(heads):
            header = jnp.where(line == 3, sections, 0.0)
            for i in range(3):
                header = jnp.where(line == i, p_ref[h : h + 1, i : i + 1], header)
            header = header.astype(BF)
            for k in range(per_head):
                c = h * per_head + k
                o_ref[c, :slice_rows, :] = s_ref[h, k * slice_rows : (k + 1) * slice_rows, :]
                o_ref[c, slice_rows + slots :, :] = header
                o_ref[c, slice_rows : slice_rows + slots, :] = q_ref[h]

    return pl.pallas_call(
        body,
        in_specs=[WHOLE] * 4,
        out_specs=WHOLE,
        out_shape=jax.ShapeDtypeStruct((count, slice_rows + slots + 8, dim), BF),
        compiler_params=pltpu.CompilerParams(vmem_limit_bytes=12 << 20),
        cost_estimate=pl.CostEstimate(flops=0, bytes_accessed=3 << 20, transcendentals=0),
    )(own_state, parts, named, queries)


def scan_and_read(got, slice_rows, slots):
    sections, _, dim = got.shape
    half = slice_rows // 2

    def body(got_ref, out_ref, states, asked_held, heads_held, ends, held, moved):
        into = ((states, 0), (heads_held, slice_rows + slots), (asked_held, slice_rows))
        arrive = [
            pltpu.make_async_copy(
                got_ref.at[:, pl.ds(first, to.shape[1]), :], to, moved.at[i]
            )
            for i, (to, first) in enumerate(into)
        ]
        for copy in arrive:
            copy.start()
        arrive[0].wait()
        arrive[1].wait()
        state = jnp.zeros((slice_rows, dim), F32)
        for c in range(sections):
            held[c, :slice_rows, :] = state.astype(BF)
            header = heads_held[c].astype(F32)
            factor = header[0:1] + header[1:2] + header[2:3]
            state = factor * state + states[c].astype(F32)
            ends[c * slice_rows : (c + 1) * slice_rows, :] = state.astype(BF)
        top = pl.ds(0, slice_rows)
        leave = [pltpu.make_async_copy(held.at[:, top, :], out_ref.at[:, top, :], moved.at[3])]
        leave[0].start()
        arrive[2].wait()
        for p in range(sections // 2):
            pair = pl.ds(2 * p, 2)
            rows = asked_held[2 * p : 2 * p + 2].reshape(2 * slots, dim)
            named = [heads_held[2 * p + k].astype(F32)[3:4, :slots] for k in range(2)]
            named = jnp.concatenate(named, axis=1)
            total = jnp.zeros((slice_rows, 2 * slots), F32)
            for j in range(0, sections, 4):
                reads = lax.dot_general(
                    ends[j * slice_rows : (j + 4) * slice_rows, :],
                    rows,
                    NT,
                    preferred_element_type=F32,
                )
                for i in range(4):
                    part = reads[i * slice_rows : (i + 1) * slice_rows]
                    total += jnp.where(named == float(j + i), part, 0.0)
            total = total.astype(BF)
            for k in range(2):
                mine = total[:, k * slots : (k + 1) * slots]
                held[2 * p + k, slice_rows:, :slots] = mine[:half]
                held[2 * p + k, slice_rows:, slots:] = mine[half:]
            below = pl.ds(slice_rows, half)
            leave.append(
                pltpu.make_async_copy(
                    held.at[pair, below, :], out_ref.at[pair, below, :], moved.at[4 + p]
                )
            )
            leave[-1].start()
        for copy in leave:
            copy.wait()

    shape = (sections, slice_rows + half, dim)
    head_rows = got.shape[1] - slice_rows - slots
    return pl.pallas_call(
        body,
        in_specs=[pl.BlockSpec(memory_space=pl.ANY)],
        out_specs=pl.BlockSpec(memory_space=pl.ANY),
        out_shape=jax.ShapeDtypeStruct(shape, BF),
        scratch_shapes=[
            pltpu.VMEM((sections, slice_rows, dim), BF),
            pltpu.VMEM((sections, slots, dim), BF),
            pltpu.VMEM((sections, head_rows, dim), BF),
            pltpu.VMEM((sections * slice_rows, dim), BF),
            pltpu.VMEM(shape, BF),
            pltpu.SemaphoreType.DMA((4 + sections // 2,)),
        ],
        compiler_params=pltpu.CompilerParams(vmem_limit_bytes=58 << 20),
        cost_estimate=pl.CostEstimate(
            flops=2 * sections * slots * sections * slice_rows * dim,
            bytes_accessed=6 << 20,
            transcendentals=0,
        ),
    )(got)


def retain(queries, within, logs, got, slice_rows, own, kept):
    sections, _, dim = got.shape
    tokens, width = queries.shape
    slots, heads = kept.shape
    per_head = sections // heads

    n = tokens + slots
    upper = n // 2

    def body(q_ref, in_ref, l_ref, got_ref, own_ref, k_ref, o_ref, t_ref, b_ref, own_held, arrived):
        fetch = pltpu.make_async_copy(own_ref, own_held, arrived)
        fetch.start()
        gains = jnp.exp(l_ref[...])
        gains = jnp.concatenate([gains] * (8 // heads), axis=0).T
        for h in range(heads):
            cols = slice(h * dim, (h + 1) * dim)
            state = got_ref[h * per_head : (h + 1) * per_head, :slice_rows, :].reshape(dim, dim)
            carried = lax.dot_general(q_ref[:, cols], state, NT, preferred_element_type=F32)
            total = in_ref[:, cols] + gains[:, h : h + 1] * carried
            o_ref[:tokens, cols] = total.astype(BF)
        fetch.wait()
        for h in range(heads):
            cols = slice(h * dim, (h + 1) * dim)
            parts = []
            for c in range(h * per_head, (h + 1) * per_head):
                held = got_ref[c, slice_rows:, :].astype(F32)
                parts += [held[:, :slots], held[:, slots:]]
            read = jnp.concatenate(parts, axis=0).T
            mixed = k_ref[:, h : h + 1] * read + own_held[:, cols]
            o_ref[tokens:, cols] = mixed.astype(BF)
        t_ref[...] = o_ref[:upper, :]
        b_ref[...] = o_ref[upper:, :]

    specs = [WHOLE] * 6
    specs[4] = pl.BlockSpec(memory_space=pl.ANY)
    return pl.pallas_call(
        body,
        in_specs=specs,
        out_specs=[WHOLE] * 3,
        out_shape=[jax.ShapeDtypeStruct((r, width), BF) for r in (n, upper, n - upper)],
        scratch_shapes=[pltpu.VMEM(own.shape, F32), pltpu.SemaphoreType.DMA],
        compiler_params=pltpu.CompilerParams(vmem_limit_bytes=12 << 20),
        cost_estimate=pl.CostEstimate(
            flops=2 * tokens * width * dim, bytes_accessed=6 << 20, transcendentals=0
        ),
    )(queries, within, logs, got, own, kept)


def gathered_projection(blocks, split, steps, w):
    me = lax.axis_index("head")
    z, x = me // 2, me % 2
    here, far = lambda d: ((z + d) % 4) * 2 + x, lambda d: ((z + d) % 4) * 2 + 1 - x
    block, top, bottom = blocks
    n, h = block.shape[0], top.shape[0]
    width = block.shape[1]
    whole = lambda slot, i: [(slot, i, 0, n, 0)]
    halves = lambda slot, i: [(slot, i, 0, h, 0), (slot, i + 1, 0, n - h, h)]

    down_top, down_bottom = down(top), down(bottom)
    from_below, from_side = up(block), across(block)
    (total,) = project(n, [block], whole(0, 0), [me], w)

    down_top, total = lax.optimization_barrier((down_top, total))
    side_below = up(after(from_side, down_bottom))
    side_top, far_bottom = across(down_top), down(down_bottom)
    side_bottom, far_top = across(after(down_bottom, from_below)), down(after(down_top, from_below))
    (total,) = project(
        total,
        [from_below, down_top, down_bottom, from_side],
        whole(0, 0) + halves(1, 1) + whole(2, 3),
        [here(-1), here(1), far(0)],
        w,
    )

    side_top, total = lax.optimization_barrier((side_top, total))
    last_top = down(side_top)
    last_bottom = across(far_bottom)
    w_last = lax.dynamic_slice_in_dim(after(w, total), far(2) * width, width, 0)
    (total,) = project(
        total,
        [side_below, far_top, far_bottom, side_top, side_bottom],
        whole(0, 0) + halves(1, 1) + halves(2, 3),
        [far(-1), here(2), far(1)],
        w,
    )
    last_top, last_bottom, total, w_last = lax.optimization_barrier(
        (last_top, last_bottom, total, w_last)
    )
    return project(total, [last_top, last_bottom], halves(0, 0), None, w_last, split, steps)


def shards(
    q_prompt,
    k_prompt,
    v_prompt,
    log_decay,
    prompt_section,
    q_step,
    k_step,
    v_step,
    step_decay,
    w_out,
):
    tokens, heads, dim = q_prompt.shape
    sections = lax.axis_size("ctx")
    rows, steps = q_step.shape[:2]

    at = jnp.arange(tokens)
    upto = (at[:, None] <= at[None, :]).astype(F32)
    cumlog = jnp.dot(log_decay, upto, precision=lax.Precision.HIGHEST)
    last_log = cumlog[:, -1]
    keys = (k_prompt.astype(F32) * jnp.exp(last_log[:, None] - cumlog).T[:, :, None]).astype(BF)
    own_state = jnp.einsum("jxp,jxa->xpa", v_prompt, keys, preferred_element_type=F32)
    total_decay = jnp.exp(last_log)
    slice_rows, slots = heads * dim // sections, rows * steps
    high = lax.reduce_precision(total_decay, 8, 7)
    middle = lax.reduce_precision(total_decay - high, 8, 7)
    parts = jnp.stack([high, middle, total_decay - high - middle], axis=1)
    asked = q_step.reshape(slots, heads, dim).transpose(1, 0, 2)
    sent = first_parcels(own_state.astype(BF), parts, prompt_section.reshape(1, rows), asked)
    got = lax.all_to_all(sent, "ctx", 0, 0)

    q_late, k_late, v_late, cum_late = after((q_prompt, k_prompt, v_prompt, cumlog), sent)
    causal = at[:, None] >= at[None, :]
    decays = jnp.where(
        causal[None], jnp.exp(jnp.minimum(cum_late[:, :, None] - cum_late[:, None, :], 0.0)), 0.0
    )
    scores = jnp.einsum("jsv,csv->sjc", q_late, k_late, preferred_element_type=F32)
    weights = (scores * decays).astype(BF)
    within = jnp.einsum("hnm,mhe->nhe", weights, v_late, preferred_element_type=F32)
    within = within.reshape(tokens, heads * dim)
    queries = q_late.reshape(tokens, heads * dim)
    got, within, queries, cum_late = lax.optimization_barrier((got, within, queries, cum_late))

    sent = scan_and_read(got, slice_rows, slots)
    got = lax.all_to_all(sent, "ctx", 0, 0)

    q_own, k_own, v_own, rates = after((q_step, k_step, v_step, step_decay), sent)
    rates = jnp.transpose(rates, (2, 1, 0))
    logs = [rates[:, 0]]
    for t in range(1, steps):
        logs.append(logs[-1] + rates[:, t])
    step_logs = jnp.stack(logs, axis=1)
    head_logs = jnp.transpose(step_logs, (0, 2, 1))
    turn = jnp.arange(steps)
    seen = turn[:, None] >= turn[None, :]
    gaps = head_logs[:, :, :, None] - head_logs[:, :, None, :]
    step_gains = jnp.where(seen[None, None], jnp.exp(jnp.minimum(gaps, 0.0)), 0.0)
    own = jnp.einsum("rthd,ruhd->rhtu", q_own, k_own, preferred_element_type=F32)
    own = jnp.einsum("rhtu,ruhe->rthe", own * step_gains, v_own.astype(F32))
    own = own.reshape(slots, heads * dim)
    kept = jnp.exp(step_logs).reshape(slots, heads)

    blocks = retain(queries, within, cum_late, got, slice_rows, own, kept)
    return tuple(gathered_projection(blocks, tokens, steps, w_out))


def solution(mesh):
    in_specs = (
        P("ctx", "head", None),
        P("ctx", "head", None),
        P("ctx", "head", None),
        P("head", "ctx"),
        P("ctx", None),
        P("ctx", None, "head", None),
        P("ctx", None, "head", None),
        P("ctx", None, "head", None),
        P("head", None, "ctx"),
        P(None, "head"),
    )
    out_specs = (P("ctx", "head"), P("ctx", None, "head"))
    return jax.shard_map(shards, mesh=mesh, in_specs=in_specs, out_specs=out_specs, check_vma=False)
```

```python
import jax
import jax.numpy as jnp
from jax import lax
from jax.experimental import pallas as pl
from jax.experimental.pallas import tpu as pltpu
from jax.sharding import PartitionSpec as P

BF, F32 = jnp.bfloat16, jnp.float32
WHOLE = pl.BlockSpec(memory_space=pltpu.VMEM)


def up(a):
    return lax.ppermute(a, "head", [(h, (h + 2) % 8) for h in range(8)])


def down(a):
    return lax.ppermute(a, "head", [(h, (h - 2) % 8) for h in range(8)])


def across(a):
    return lax.ppermute(a, "head", [(h, h ^ 1) for h in range(8)])


def after(values, *others):
    return lax.optimization_barrier((values, others))[0]


def project(total, srcs, terms, heads, w, split=None, steps=None):
    width, columns = srcs[0].shape[1], w.shape[1]
    n_slot = 0 if heads is None else len(heads)
    old = [] if isinstance(total, int) else [total]
    rows = total if isinstance(total, int) else total.shape[0]

    def add(slot, weights, src_refs, old_refs, out_refs):
        for s, i, s0, n, a0 in terms:
            if s != slot:
                continue
            part = jnp.dot(src_refs[i][s0 : s0 + n, :], weights, preferred_element_type=F32)
            if slot:
                part += out_refs[0][a0 : a0 + n, :]
            elif old:
                part += old_refs[0][a0 : a0 + n, :]
            if split is None:
                out_refs[0][a0 : a0 + n, :] = part
                continue
            top = min(max(split - a0, 0), n)
            if top:
                out_refs[0][a0 : a0 + top, :] = part[:top].astype(BF)
            if top < n:
                below = a0 + top - split
                first, some = below // steps, (n - top) // steps
                rest = part[top:].reshape(some, steps, columns)
                out_refs[1][first : first + some] = rest.astype(BF)

    def body(*refs):
        if heads is None:
            src_refs, w_ref, refs = refs[: len(srcs)], refs[len(srcs)], refs[len(srcs) + 1 :]
            add(0, w_ref[...], src_refs, refs[: len(old)], refs[len(old) :])
            return
        heads_ref, *refs = refs
        src_refs, w_ref, refs = refs[: len(srcs)], refs[len(srcs)], refs[len(srcs) + 1 :]
        w_held, arrived = refs[-2:]
        copies = []
        for slot in range(n_slot):
            first = pl.multiple_of(heads_ref[slot] * width, width)
            copies.append(
                pltpu.make_async_copy(
                    w_ref.at[pl.ds(first, width), :], w_held.at[slot], arrived.at[slot]
                )
            )
            copies[-1].start()
        for slot in range(n_slot):
            copies[slot].wait()
            add(slot, w_held[slot], src_refs, refs[: len(old)], refs[len(old) : -2])

    if split is None:
        out = [jax.ShapeDtypeStruct((rows, columns), F32)]
    else:
        shapes = (split, columns), ((rows - split) // steps, steps, columns)
        out = [jax.ShapeDtypeStruct(shape, BF) for shape in shapes]
    flops = sum(2 * t[3] * width * columns for t in terms)
    cost = pl.CostEstimate(
        flops=flops >> 10, bytes_accessed=1 << 10, transcendentals=0
    )
    if heads is None:
        return pl.pallas_call(
            body,
            in_specs=[WHOLE] * (len(srcs) + 1 + len(old)),
            out_specs=[WHOLE] * len(out),
            out_shape=out,
            compiler_params=pltpu.CompilerParams(vmem_limit_bytes=16 << 20),
            cost_estimate=cost,
        )(*srcs, w, *old)
    return pl.pallas_call(
        body,
        in_specs=[pl.BlockSpec(memory_space=pltpu.SMEM)]
        + [WHOLE] * len(srcs)
        + [pl.BlockSpec(memory_space=pltpu.HBM)]
        + [WHOLE] * len(old),
        out_specs=[WHOLE] * len(out),
        out_shape=out,
        scratch_shapes=[
            pltpu.VMEM((n_slot, width, columns), BF),
            pltpu.SemaphoreType.DMA((n_slot,)),
        ],
        compiler_params=pltpu.CompilerParams(vmem_limit_bytes=42 << 20),
        cost_estimate=cost,
    )(jnp.stack(heads).astype(jnp.int32), *srcs, w, *old)


NT = (((1,), (1,)), ((), ()))


def first_parcels(own_state, parts, named, queries):
    heads, dim, _ = own_state.shape
    slots, rows = queries.shape[0], named.shape[1]
    count = lax.axis_size("ctx")
    per_head = count // heads
    slice_rows = heads * dim // count

    def body(s_ref, p_ref, n_ref, q_ref, o_ref):
        row = lax.broadcasted_iota(jnp.int32, (rows, slots), 0)
        lane = lax.broadcasted_iota(jnp.int32, (rows, slots), 1)
        first = row * (slots // rows)
        mine = (lane >= first) & (lane < first + slots // rows)
        sections = jnp.broadcast_to(n_ref[...].astype(F32), (8, rows)).astype(BF)
        sections = jnp.dot(sections, mine.astype(BF), preferred_element_type=F32)[:1]
        sections = jnp.concatenate([sections, jnp.zeros((1, dim - slots), F32)], axis=1)
        line = lax.broadcasted_iota(jnp.int32, (8, dim), 0)
        for h in range(heads):
            asked = q_ref[:, h, :]
            header = jnp.where(line == 3, sections, 0.0)
            for i in range(3):
                header = jnp.where(line == i, p_ref[h : h + 1, i : i + 1], header)
            header = header.astype(BF)
            for k in range(per_head):
                c = h * per_head + k
                o_ref[c, :slice_rows, :] = s_ref[h, k * slice_rows : (k + 1) * slice_rows, :]
                o_ref[c, slice_rows + slots :, :] = header
                o_ref[c, slice_rows : slice_rows + slots, :] = asked

    return pl.pallas_call(
        body,
        in_specs=[WHOLE] * 4,
        out_specs=WHOLE,
        out_shape=jax.ShapeDtypeStruct((count, slice_rows + slots + 8, dim), BF),
        compiler_params=pltpu.CompilerParams(vmem_limit_bytes=12 << 20),
        cost_estimate=pl.CostEstimate(flops=0, bytes_accessed=3 << 20, transcendentals=0),
    )(own_state, parts, named, queries)


def scan_and_read(got, slice_rows, slots):
    sections, _, dim = got.shape
    half = slice_rows // 2

    def body(got_ref, out_ref, states, asked_held, heads_held, ends, held, moved):
        into = ((states, 0), (heads_held, slice_rows + slots), (asked_held, slice_rows))
        arrive = [
            pltpu.make_async_copy(
                got_ref.at[:, pl.ds(first, to.shape[1]), :], to, moved.at[i]
            )
            for i, (to, first) in enumerate(into)
        ]
        for copy in arrive:
            copy.start()
        arrive[0].wait()
        arrive[1].wait()
        state = jnp.zeros((slice_rows, dim), F32)
        for c in range(sections):
            held[c, :slice_rows, :] = state.astype(BF)
            header = heads_held[c].astype(F32)
            factor = header[0:1] + header[1:2] + header[2:3]
            state = factor * state + states[c].astype(F32)
            ends[c * slice_rows : (c + 1) * slice_rows, :] = state.astype(BF)
        top = pl.ds(0, slice_rows)
        leave = [pltpu.make_async_copy(held.at[:, top, :], out_ref.at[:, top, :], moved.at[3])]
        leave[0].start()
        arrive[2].wait()
        for p in range(sections // 2):
            pair = pl.ds(2 * p, 2)
            rows = asked_held[2 * p : 2 * p + 2].reshape(2 * slots, dim)
            named = [heads_held[2 * p + k].astype(F32)[3:4, :slots] for k in range(2)]
            named = jnp.concatenate(named, axis=1)
            total = jnp.zeros((slice_rows, 2 * slots), F32)
            for j in range(0, sections, 4):
                reads = lax.dot_general(
                    ends[j * slice_rows : (j + 4) * slice_rows, :],
                    rows,
                    NT,
                    preferred_element_type=F32,
                )
                for i in range(4):
                    part = reads[i * slice_rows : (i + 1) * slice_rows]
                    total += jnp.where(named == float(j + i), part, 0.0)
            total = total.astype(BF)
            for k in range(2):
                mine = total[:, k * slots : (k + 1) * slots]
                held[2 * p + k, slice_rows:, :slots] = mine[:half]
                held[2 * p + k, slice_rows:, slots:] = mine[half:]
            below = pl.ds(slice_rows, half)
            leave.append(
                pltpu.make_async_copy(
                    held.at[pair, below, :], out_ref.at[pair, below, :], moved.at[4 + p]
                )
            )
            leave[-1].start()
        for copy in leave:
            copy.wait()

    shape = (sections, slice_rows + half, dim)
    head_rows = got.shape[1] - slice_rows - slots
    return pl.pallas_call(
        body,
        in_specs=[pl.BlockSpec(memory_space=pl.ANY)],
        out_specs=pl.BlockSpec(memory_space=pl.ANY),
        out_shape=jax.ShapeDtypeStruct(shape, BF),
        scratch_shapes=[
            pltpu.VMEM((sections, slice_rows, dim), BF),
            pltpu.VMEM((sections, slots, dim), BF),
            pltpu.VMEM((sections, head_rows, dim), BF),
            pltpu.VMEM((sections * slice_rows, dim), BF),
            pltpu.VMEM(shape, BF),
            pltpu.SemaphoreType.DMA((4 + sections // 2,)),
        ],
        compiler_params=pltpu.CompilerParams(vmem_limit_bytes=58 << 20),
        cost_estimate=pl.CostEstimate(
            flops=2 * sections * slots * sections * slice_rows * dim,
            bytes_accessed=6 << 20,
            transcendentals=0,
        ),
    )(got)


def retain(queries, within, logs, got, slice_rows, own, kept):
    sections, _, dim = got.shape
    tokens, width = queries.shape
    slots, heads = kept.shape
    per_head = sections // heads

    n = tokens + slots
    upper = n // 2

    def body(q_ref, in_ref, l_ref, got_ref, own_ref, k_ref, o_ref, t_ref, b_ref, own_held, arrived):
        fetch = pltpu.make_async_copy(own_ref, own_held, arrived)
        fetch.start()
        gains = jnp.exp(l_ref[...])
        gains = jnp.concatenate([gains] * (8 // heads), axis=0).T
        for h in range(heads):
            cols = slice(h * dim, (h + 1) * dim)
            state = got_ref[h * per_head : (h + 1) * per_head, :slice_rows, :].reshape(dim, dim)
            carried = lax.dot_general(q_ref[:, cols], state, NT, preferred_element_type=F32)
            total = in_ref[:, cols] + gains[:, h : h + 1] * carried
            o_ref[:tokens, cols] = total.astype(BF)
        fetch.wait()
        for h in range(heads):
            cols = slice(h * dim, (h + 1) * dim)
            parts = []
            for c in range(h * per_head, (h + 1) * per_head):
                held = got_ref[c, slice_rows:, :].astype(F32)
                parts += [held[:, :slots], held[:, slots:]]
            read = jnp.concatenate(parts, axis=0).T
            mixed = k_ref[:, h : h + 1] * read + own_held[:, cols]
            o_ref[tokens:, cols] = mixed.astype(BF)
        t_ref[...] = o_ref[:upper, :]
        b_ref[...] = o_ref[upper:, :]

    specs = [WHOLE] * 6
    specs[4] = pl.BlockSpec(memory_space=pl.ANY)
    return pl.pallas_call(
        body,
        in_specs=specs,
        out_specs=[WHOLE] * 3,
        out_shape=[jax.ShapeDtypeStruct((r, width), BF) for r in (n, upper, n - upper)],
        scratch_shapes=[pltpu.VMEM(own.shape, F32), pltpu.SemaphoreType.DMA],
        compiler_params=pltpu.CompilerParams(vmem_limit_bytes=12 << 20),
        cost_estimate=pl.CostEstimate(
            flops=2 * tokens * width * dim, bytes_accessed=6 << 20, transcendentals=0
        ),
    )(queries, within, logs, got, own, kept)


def gathered_projection(blocks, split, steps, w):
    me = lax.axis_index("head")
    z, x = me // 2, me % 2
    here, far = lambda d: ((z + d) % 4) * 2 + x, lambda d: ((z + d) % 4) * 2 + 1 - x
    block, top, bottom = blocks
    n, h = block.shape[0], top.shape[0]
    width = block.shape[1]
    whole = lambda slot, i: [(slot, i, 0, n, 0)]
    halves = lambda slot, i: [(slot, i, 0, h, 0), (slot, i + 1, 0, n - h, h)]

    down_top, down_bottom = down(top), down(bottom)
    from_below, from_side = up(block), across(block)
    (total,) = project(n, [block], whole(0, 0), [me], w)

    down_top, total = lax.optimization_barrier((down_top, total))
    side_below = up(after(from_side, down_bottom))
    side_top, far_bottom = across(down_top), down(down_bottom)
    side_bottom, far_top = across(after(down_bottom, from_below)), down(after(down_top, from_below))
    (total,) = project(
        total,
        [from_below, down_top, down_bottom, from_side],
        whole(0, 0) + halves(1, 1) + whole(2, 3),
        [here(-1), here(1), far(0)],
        w,
    )

    side_top, total = lax.optimization_barrier((side_top, total))
    last_top = down(side_top)
    last_bottom = across(far_bottom)
    w_last = lax.dynamic_slice_in_dim(after(w, total), far(2) * width, width, 0)
    (total,) = project(
        total,
        [side_below, far_top, far_bottom, side_top, side_bottom],
        whole(0, 0) + halves(1, 1) + halves(2, 3),
        [far(-1), here(2), far(1)],
        w,
    )
    last_top, last_bottom, total, w_last = lax.optimization_barrier(
        (last_top, last_bottom, total, w_last)
    )
    return project(total, [last_top, last_bottom], halves(0, 0), None, w_last, split, steps)


def shards(
    q_prompt,
    k_prompt,
    v_prompt,
    log_decay,
    prompt_section,
    q_step,
    k_step,
    v_step,
    step_decay,
    w_out,
):
    tokens, heads, dim = q_prompt.shape
    sections = lax.axis_size("ctx")
    rows, steps = q_step.shape[:2]

    at = jnp.arange(tokens)
    upto = (at[:, None] <= at[None, :]).astype(F32)
    cumlog = jnp.dot(log_decay, upto, precision=lax.Precision.HIGHEST)
    last_log = cumlog[:, -1]
    keys = (k_prompt.astype(F32) * jnp.exp(last_log[:, None] - cumlog).T[:, :, None]).astype(BF)
    own_state = jnp.einsum("jxp,jxa->xpa", v_prompt, keys, preferred_element_type=F32)
    total_decay = jnp.exp(last_log)
    slice_rows, slots = heads * dim // sections, rows * steps
    high = lax.reduce_precision(total_decay, 8, 7)
    middle = lax.reduce_precision(total_decay - high, 8, 7)
    parts = jnp.stack([high, middle, total_decay - high - middle], axis=1)
    asked = q_step.reshape(slots, heads, dim)
    sent = first_parcels(own_state.astype(BF), parts, prompt_section.reshape(1, rows), asked)
    got = lax.all_to_all(sent, "ctx", 0, 0)

    q_late, k_late, v_late, cum_late = after((q_prompt, k_prompt, v_prompt, cumlog), sent)
    causal = at[:, None] >= at[None, :]
    decays = jnp.where(
        causal[None], jnp.exp(jnp.minimum(cum_late[:, :, None] - cum_late[:, None, :], 0.0)), 0.0
    )
    scores = jnp.einsum("jsv,csv->sjc", q_late, k_late, preferred_element_type=F32)
    weights = (scores * decays).astype(BF)
    within = jnp.einsum("hnm,mhe->nhe", weights, v_late, preferred_element_type=F32)
    within = within.reshape(tokens, heads * dim)
    queries = q_late.reshape(tokens, heads * dim)
    got, within, queries, cum_late = lax.optimization_barrier((got, within, queries, cum_late))

    sent = scan_and_read(got, slice_rows, slots)
    got = lax.all_to_all(sent, "ctx", 0, 0)

    q_own, k_own, v_own, rates = after((q_step, k_step, v_step, step_decay), sent)
    rates = jnp.transpose(rates, (2, 1, 0))
    logs = [rates[:, 0]]
    for t in range(1, steps):
        logs.append(logs[-1] + rates[:, t])
    step_logs = jnp.stack(logs, axis=1)
    head_logs = jnp.transpose(step_logs, (0, 2, 1))
    turn = jnp.arange(steps)
    seen = turn[:, None] >= turn[None, :]
    gaps = head_logs[:, :, :, None] - head_logs[:, :, None, :]
    step_gains = jnp.where(seen[None, None], jnp.exp(jnp.minimum(gaps, 0.0)), 0.0)
    own = jnp.einsum("rthd,ruhd->rhtu", q_own, k_own, preferred_element_type=F32)
    own = jnp.einsum("rhtu,ruhe->rthe", own * step_gains, v_own.astype(F32))
    own = own.reshape(slots, heads * dim)
    kept = jnp.exp(step_logs).reshape(slots, heads)

    blocks = retain(queries, within, cum_late, got, slice_rows, own, kept)
    return tuple(gathered_projection(blocks, tokens, steps, w_out))


def solution(mesh):
    in_specs = (
        P("ctx", "head", None),
        P("ctx", "head", None),
        P("ctx", "head", None),
        P("head", "ctx"),
        P("ctx", None),
        P("ctx", None, "head", None),
        P("ctx", None, "head", None),
        P("ctx", None, "head", None),
        P("head", None, "ctx"),
        P(None, "head"),
    )
    out_specs = (P("ctx", "head"), P("ctx", None, "head"))
    return jax.shard_map(shards, mesh=mesh, in_specs=in_specs, out_specs=out_specs, check_vma=False)
```
